32 devices in a mesh: pipe: 4 (over y, x), ctx: 2 (over core), tp: 4 (over z).
Axes of the slice: x: 2, y: 2, z: 4, core: 2. Of those that a mesh axis runs over, the one named last changes fastest.
Arguments:
- mamba_input: bfloat16 [4, 768, 8192], P('pipe', 'ctx', 'tp'), may hold values from -6 to 6
- mamba_bc: bfloat16 [4, 768, 2, 512], P('pipe', 'ctx', None, 'tp'), may hold values from -6 to 6
- gate_input: bfloat16 [4, 768, 8192], P('pipe', 'ctx', 'tp'), may hold values from -6 to 6
- step_input: bfloat16 [4, 768, 128], P('pipe', 'ctx', 'tp'), may hold values from -4 to 4
- step_bias: float32 [4, 128], P('pipe', 'tp'), may hold values from -1 to 1
- decay_rate: float32 [4, 128], P('pipe', 'tp'), may hold values from 6.510417e-05 to 0.03
- skip_gain: float32 [4, 128], P('pipe', 'tp'), may hold values from 0.5 to 1.5
- conv_weight: float32 [4, 4, 8192], P('pipe', None, 'tp'), may hold values from -3 to 3
- conv_bc_weight: float32 [4, 4, 2, 512], P('pipe', None, None, 'tp'), may hold values from -3 to 3
- norm_gain: float32 [4, 8192], P('pipe', 'tp'), may hold values from 0.5 to 1.5
- queries: bfloat16 [4, 768, 4096], P('pipe', 'ctx', 'tp'), may hold values from -160 to 160
- attn_keys: bfloat16 [4, 768, 512], P('pipe', 'ctx', 'tp'), may hold values from -7 to 7
- attn_values: bfloat16 [4, 768, 512], P('pipe', 'ctx', 'tp'), may hold values from -6 to 6
- documents: int32 [4, 768], P('pipe'), may hold values from 0 to 3, never falling along the last dimension, each value on 1 to 384 neighbouring positions
Outputs:
- mixer_out: bfloat16 [4, 768, 8192], P('pipe', 'ctx', 'tp')
- attn_out: bfloat16 [4, 768, 4096], P('pipe', 'ctx', 'tp')
The draws below stay inside these ranges and needn't reach their ends.
All inputs are finite; a program needn't handle non-finite values.
Results may differ from the reference program's by a relative error of at most 0.0035.
Values may be sent and summed in bfloat16 or wider, within the bound.
A program may use at most 64 MiB of HBM per device.

```python
import math
import jax
import jax.numpy as jnp
import numpy as np
from jax import lax

HEADS = 128
HDIM = 64
STATE = 128
GROUPS = 4
KERNEL = 4
QHEADS = 32
KVHEADS = 4
ADIM = 128
DOCS = 4
TOK_DEV = 384
INNER = 8192
TOKENS = 768
SECTIONS = 4


def query_key_pair(key):
    key_seed = jax.random.fold_in(key, 101)
    query_seed = jax.random.fold_in(key, 102)
    keys_all = jnp.clip(jax.random.normal(key_seed, (SECTIONS, TOKENS, KVHEADS, ADIM), jnp.float32), -6.0, 6.0)
    queries_all = jnp.clip(jax.random.normal(query_seed, (SECTIONS, TOKENS, QHEADS, ADIM), jnp.float32), -6.0, 6.0)
    return (queries_all.reshape(SECTIONS, TOKENS, QHEADS * ADIM), keys_all.reshape(SECTIONS, TOKENS, KVHEADS * ADIM))


def draw_queries(key, part):
    return query_key_pair(key)[0].astype(jnp.bfloat16)


def draw_attn_keys(key, part):
    return query_key_pair(key)[1].astype(jnp.bfloat16)


def block_levels(stream_key, shape, cuts, least, largest):
    gain, own = 1.0, jax.random.fold_in(stream_key, 6)
    for dim, parts in cuts:
        heights = jnp.exp(jax.random.uniform(jax.random.fold_in(own, dim), (parts,), jnp.float32, least / len(cuts), largest / len(cuts)))
        gain = gain * jnp.repeat(heights, shape[dim] // parts).reshape([-1 if axis == dim else 1 for axis in range(len(shape))])
    return gain


def profile(number_of, total, reach, lean):
    loads = [(1 << 20) // math.isqrt(rank ** lean) + 1 for rank in range(2, number_of + 1)]
    spare, given = total - reach - (number_of - 1), [1] * (number_of - 1)
    while spare > 0:
        candidates = [i for i in range(number_of - 1) if given[i] < reach]
        pool, left = sum([loads[i] for i in candidates]), spare
        for i in candidates:
            addition = min(reach - given[i], max(1, left * loads[i] // pool), spare)
            given[i] = given[i] + addition
            spare = spare - addition
    return np.array([reach] + given)


def ragged_sizes(key, number_of, total, most, slope):
    if number_of == 2:
        one = jax.random.randint(key, (), max(1, total - most), min(most, total - 1) + 1)
        return jnp.stack([one, total - one])
    tallies = jnp.asarray(profile(number_of, total, most, slope), jnp.int32)
    couples = (number_of - 1) // 2
    source_of, receiver = tallies[1:1 + 2 * couples:2], tallies[2:2 + 2 * couples:2]
    room = jnp.minimum(source_of - 1, most - receiver)
    moved = jax.random.randint(jax.random.fold_in(key, 1), (couples,), 0, 1 << 20) % (room + 1)
    tallies = tallies.at[1:1 + 2 * couples:2].set(source_of - moved).at[2:2 + 2 * couples:2].set(receiver + moved)
    return tallies[jax.random.permutation(jax.random.fold_in(key, 2), number_of)]


def centred(rng, dims, deviation, bound, cuts=(), held_as=jnp.bfloat16):
    loudness = block_levels(rng, dims, cuts, -0.22, 0.18) if cuts else 1.0
    values = jax.random.normal(rng, dims, jnp.float32) * deviation * loudness
    return jnp.minimum(jnp.maximum(values, -bound), bound).astype(held_as)


def setup_inputs(seed: int = 0) -> dict:
    arg_keys = jax.random.split(jax.random.key(seed), 15)
    return {
        "mamba_input": centred(arg_keys[0], (SECTIONS, TOKENS, INNER), 1.0, 6.0, ((0, 4), (1, 2), (2, 4))),
        "mamba_bc": centred(arg_keys[1], (SECTIONS, TOKENS, 2, GROUPS * STATE), 1.0, 6.0, ((0, 4), (1, 2), (3, 4))),
        "gate_input": centred(arg_keys[2], (SECTIONS, TOKENS, INNER), 1.0, 6.0, ((0, 4), (1, 2), (2, 4))),
        "step_input": centred(arg_keys[3], (SECTIONS, TOKENS, HEADS), 1.0, 4.0, ((0, 4), (1, 2), (2, 4))),
        "step_bias": jnp.clip(jax.random.uniform(arg_keys[4], (SECTIONS, HEADS), jnp.float32, -1.0, 1.0) * block_levels(arg_keys[4], (SECTIONS, HEADS), ((0, 4), (1, 4)), -0.4, 0.0), -1.0, 1.0),
        "decay_rate": jnp.clip(jnp.exp(math.log(0.03) - 6.132964 * jax.random.uniform(arg_keys[5], (SECTIONS, HEADS), jnp.float32) ** block_levels(arg_keys[5], (SECTIONS, HEADS), ((0, 4), (1, 4)), -0.2, 0.2)), 6.510417006211355e-05, 0.03),
        "skip_gain": jnp.clip(0.5 + 1.0 * jax.random.uniform(arg_keys[6], (SECTIONS, HEADS), jnp.float32) ** block_levels(arg_keys[6], (SECTIONS, HEADS), ((0, 4), (1, 4)), -0.2, 0.2), 0.5, 1.5),
        "conv_weight": centred(arg_keys[7], (SECTIONS, KERNEL, INNER), KERNEL ** -0.5, 3.0, ((0, 4), (2, 4)), jnp.float32),
        "conv_bc_weight": centred(arg_keys[8], (SECTIONS, KERNEL, 2, GROUPS * STATE), KERNEL ** -0.5, 3.0, ((0, 4), (3, 4)), jnp.float32),
        "norm_gain": jnp.clip(1.0 + 0.1 * jax.random.normal(arg_keys[9], (SECTIONS, INNER), jnp.float32), 0.5, 1.5),
        "queries": draw_queries(jax.random.fold_in(arg_keys[14], 71), 0),
        "attn_keys": draw_attn_keys(jax.random.fold_in(arg_keys[14], 71), 0),
        "attn_values": centred(arg_keys[12], (SECTIONS, TOKENS, KVHEADS * ADIM), 1.0, 6.0, ((0, 4), (1, 2), (2, 4))),
        "documents": jax.vmap(lambda own: jnp.searchsorted(jnp.cumsum(ragged_sizes(own, DOCS, TOKENS, TOKENS // 2, 1)), jnp.arange(TOKENS), side="right"))(jax.random.split(arg_keys[13], SECTIONS)).reshape((SECTIONS, TOKENS)).astype(jnp.int32),
    }


highest = lax.Precision.HIGHEST

def conv_silu(padded, weight, length):
    summed = jnp.zeros((length,) + padded.shape[1:], jnp.float32)
    for offset in range(weight.shape[0]):
        summed = summed + weight[offset] * padded[offset:offset + length].astype(jnp.float32)
    return jax.nn.silu(summed)

def local_scan(x_block, b_block, c_block, step_block, log_block, groups):
    length, head_count, head_size = x_block.shape
    per_group = head_count // groups
    cumulative = jnp.cumsum(log_block, axis=0)
    gram_matrix = jnp.einsum('tgn,sgn->gts', c_block, b_block, precision=highest)
    spread = cumulative.T[:, :, None] - cumulative.T[:, None, :]
    row_index = lax.broadcasted_iota(jnp.int32, (length, length), 0)
    col_index = lax.broadcasted_iota(jnp.int32, (length, length), 1)
    decays = jnp.exp(jnp.where(row_index >= col_index, spread, -jnp.inf))
    weights = decays.reshape(groups, per_group, length, length) * gram_matrix[:, None] * step_block.T.reshape(groups, per_group, 1, length)
    inside = jnp.einsum('ghts,sghp->tghp', weights, x_block.reshape(length, groups, per_group, head_size), precision=highest)
    inside = inside.reshape(length, head_count, head_size)
    end_log = cumulative[-1]
    tail_decay = jnp.exp(end_log[None, :] - cumulative) * step_block
    weighted = (x_block * tail_decay[:, :, None]).reshape(length, groups, per_group, head_size)
    contrib = jnp.einsum('tgn,tghp->ghpn', b_block, weighted, precision=highest).reshape(head_count, head_size, -1)
    return (inside, contrib, jnp.exp(end_log), cumulative)

def incoming_term(c_block, carried, cumulative, groups):
    length, head_count = cumulative.shape
    head_size = carried.shape[1]
    per_group = head_count // groups
    grid = carried.reshape(groups, per_group, head_size, -1)
    result = jnp.einsum('tgn,ghpn->tghp', c_block, grid, precision=highest).reshape(length, head_count, head_size)
    return result * jnp.exp(cumulative)[:, :, None]

def gated_norm(ssd_out, gate_in, gain_in, groups):
    gated_out = ssd_out * jax.nn.silu(gate_in.astype(jnp.float32))
    row_count, width = gated_out.shape
    grouped = gated_out.reshape(row_count, groups, width // groups)
    mean_square = lax.optimization_barrier(jnp.mean(grouped * grouped, axis=-1, keepdims=True))
    normed = (grouped * lax.rsqrt(mean_square + 1e-05)).reshape(row_count, width)
    return (normed * gain_in).astype(jnp.bfloat16)

def mamba_section(mamba_input, mamba_bc, gate_input, step_input, step_bias, decay_rate, skip_gain, conv_weight, conv_bc_weight, norm_gain):
    margin = KERNEL - 1
    x_padded = jnp.concatenate([jnp.zeros((margin, INNER), mamba_input.dtype), mamba_input], 0)
    x_conv = conv_silu(x_padded, conv_weight, TOKENS)
    bc_padded = jnp.concatenate([jnp.zeros((margin, 2, GROUPS * STATE), mamba_bc.dtype), mamba_bc], 0)
    bc_conv = conv_silu(bc_padded, conv_bc_weight, TOKENS)
    step_size = jax.nn.softplus(step_input.astype(jnp.float32) + step_bias)
    log_decay = -decay_rate * step_size
    blocks = TOKENS // TOK_DEV
    x_blocks = x_conv.reshape(blocks, TOK_DEV, HEADS, HDIM)
    b_blocks = bc_conv[:, 0].reshape(blocks, TOK_DEV, GROUPS, STATE)
    c_blocks = bc_conv[:, 1].reshape(blocks, TOK_DEV, GROUPS, STATE)
    step_blocks = step_size.reshape(blocks, TOK_DEV, HEADS)
    log_blocks = log_decay.reshape(blocks, TOK_DEV, HEADS)

    def advance(carried, pieces):
        x_block, b_block, c_block, step_block, log_block = pieces
        inside, contrib, shard_decay, cumulative = local_scan(x_block, b_block, c_block, step_block, log_block, GROUPS)
        incoming_part = incoming_term(c_block, carried, cumulative, GROUPS)
        output = inside + incoming_part + skip_gain[None, :, None] * x_block
        return (shard_decay[:, None, None] * carried + contrib, output)
    initial = jnp.zeros((HEADS, HDIM, STATE), jnp.float32)
    unused, outputs = lax.scan(advance, initial, (x_blocks, b_blocks, c_blocks, step_blocks, log_blocks))
    ssd_out = outputs.reshape(TOKENS, INNER)
    return gated_norm(ssd_out, gate_input, norm_gain, GROUPS)

def attend_section(queries, attn_keys, attn_values, documents):
    per_kv = QHEADS // KVHEADS
    logit_scale = 1.0 / math.sqrt(ADIM)
    key_widened = attn_keys.astype(jnp.float32).reshape(TOKENS, KVHEADS, ADIM)
    value_widened = attn_values.astype(jnp.float32).reshape(TOKENS, KVHEADS, ADIM)
    positions = jnp.arange(TOKENS, dtype=jnp.int32)
    blocks = TOKENS // TOK_DEV
    query_blocks = queries.reshape(blocks, TOK_DEV, KVHEADS, per_kv, ADIM)

    def one_block(pieces):
        query_tile, first_row = pieces
        query_pos = first_row + jnp.arange(TOK_DEV, dtype=jnp.int32)
        query_doc = lax.dynamic_slice_in_dim(documents, first_row, TOK_DEV)
        attention_logits = jnp.einsum('hbau,zbu->bahz', query_tile.astype(jnp.float32), key_widened) * logit_scale
        allowed = (positions[None, :] <= query_pos[:, None]) & (documents[None, :] == query_doc[:, None])
        masked = jnp.where(allowed, attention_logits, -1e+30)
        row_max = lax.optimization_barrier(jnp.max(masked, axis=-1, keepdims=True))
        weights_exp = jnp.where(allowed, jnp.exp(masked - row_max), 0.0)
        row_sum_running = lax.optimization_barrier(jnp.sum(weights_exp, axis=-1))
        rounded_result = lax.optimization_barrier(weights_exp.astype(jnp.bfloat16)).astype(jnp.float32)
        mixer_result = jnp.einsum('ljnx,xlc->ljnc', rounded_result, value_widened) / row_sum_running[..., None]
        return mixer_result.transpose(2, 0, 1, 3).reshape(TOK_DEV, QHEADS * ADIM).astype(jnp.bfloat16)
    starts = jnp.arange(blocks, dtype=jnp.int32) * TOK_DEV
    result = lax.map(one_block, (query_blocks, starts))
    return result.reshape(TOKENS, QHEADS * ADIM)

def reference(mamba_input, mamba_bc, gate_input, step_input, step_bias, decay_rate, skip_gain, conv_weight, conv_bc_weight, norm_gain, queries, attn_keys, attn_values, documents):
    mixers = []
    attended_list = []
    for section_index in range(SECTIONS):
        mixers.append(mamba_section(mamba_input[section_index], mamba_bc[section_index], gate_input[section_index], step_input[section_index], step_bias[section_index], decay_rate[section_index], skip_gain[section_index], conv_weight[section_index], conv_bc_weight[section_index], norm_gain[section_index]))
        attended_list.append(attend_section(queries[section_index], attn_keys[section_index], attn_values[section_index], documents[section_index]))
    return (jnp.roll(jnp.stack(mixers), 1, axis=0), jnp.roll(jnp.stack(attended_list), 1, axis=0))
```

```python
import functools
import math

import jax
import jax.numpy as jnp
from jax import lax
from jax.experimental import pallas as pl
from jax.experimental.pallas import tpu as pltpu
from jax.sharding import PartitionSpec as P

HDIM = 64
STATE = 128
KERNEL = 4
ADIM = 128
HALO = 16
LANES = 256
ROWS = 128
PAIR = 2 * ADIM
MESH = pl.DeviceIdType.MESH
highest = lax.Precision.HIGHEST


def silu(v):
    return v / (1.0 + jnp.exp(-v))


def split2(v):
    high = v.astype(jnp.bfloat16)
    return high, (v - high.astype(jnp.float32)).astype(jnp.bfloat16)


def split3(v):
    high = v.astype(jnp.bfloat16)
    rest = v - high.astype(jnp.float32)
    mid = rest.astype(jnp.bfloat16)
    low = (rest - mid.astype(jnp.float32)).astype(jnp.bfloat16)
    return jnp.concatenate([high, mid, low], axis=1)


def mm(a, b):
    return jnp.dot(a, b, preferred_element_type=jnp.float32)


def nt(a, b, precision=None):
    return lax.dot_general(
        a, b, (((1,), (1,)), ((), ())), precision=precision, preferred_element_type=jnp.float32
    )


def kernel(
    n_ctx,
    n_pipe,
    x_hbm,
    bc_hbm,
    z_hbm,
    step_hbm,
    bias_hbm,
    rate_hbm,
    skip_hbm,
    cw_hbm,
    cbw_hbm,
    gain_hbm,
    q_hbm,
    k_hbm,
    v_hbm,
    doc_hbm,
    mix_out,
    attn_out,
    x_ref,
    bc_ref,
    z_ref,
    step_ref,
    bias_ref,
    rate_ref,
    skip_ref,
    cw_ref,
    cbw_ref,
    gain_ref,
    q_ref,
    doc_ref,
    load_sem,
    kv_scr,
    halo_x,
    halo_bc,
    state_in,
    state_out,
    attn_scr,
    mix_scr,
    mask_scr,
    expand,
    x_ext,
    bc_ext,
    xc_scr,
    xt_hi,
    xt_lo,
    g_hi,
    g_lo,
    state_acc,
    gated,
    kv_send,
    kv_recv,
    halo_send,
    halo_recv,
    st_send,
    st_recv,
    at_send,
    at_recv,
    mx_send,
    mx_recv,
):
    me = lax.axis_index("ctx")
    stage = lax.axis_index("pipe")
    following = lax.rem(stage + 1, n_pipe)
    previous = lax.rem(stage + n_pipe - 1, n_pipe)
    rows, width = x_ref.shape
    pairs = q_ref.shape[1] // PAIR
    blocks = rows // ROWS
    window = doc_ref.shape[1] // 2
    own = (n_ctx - 1) * rows

    local_keys = pl.ds(own, rows)
    sources = (x_hbm, bc_hbm, z_hbm, step_hbm, bias_hbm, rate_hbm, skip_hbm)
    sources += (cw_hbm, cbw_hbm, gain_hbm, k_hbm, v_hbm, doc_hbm)
    targets = (x_ref, bc_ref, z_ref, step_ref, bias_ref, rate_ref, skip_ref, cw_ref, cbw_ref, gain_ref)
    targets += (kv_scr.at[0, local_keys], kv_scr.at[1, local_keys], doc_ref)
    for r in range(blocks):
        part = pl.ds(r * ROWS, ROWS)
        sources += (q_hbm.at[part],)
        targets += (q_ref.at[part],)
    loads = [
        pltpu.make_async_copy(source, target, load_sem.at[i])
        for i, (source, target) in enumerate(zip(sources, targets))
    ]
    queries_at = 13
    for i in (12, 10, 11, *range(queries_at, queries_at + blocks), 0, 1, 3, 4, 5, 6, 7, 8, 9, 2):
        loads[i].start()

    barrier = pltpu.get_barrier_semaphore()
    pl.semaphore_signal(barrier, inc=1, device_id={"pipe": following}, device_id_type=MESH)
    pl.semaphore_signal(barrier, inc=1, device_id={"pipe": previous}, device_id_type=MESH)
    for d in range(1, n_ctx):
        pl.semaphore_signal(
            barrier, inc=1, device_id={"ctx": lax.rem(me + d, n_ctx)}, device_id_type=MESH
        )
    def kv_copy(d, which):
        return pltpu.make_async_remote_copy(
            src_ref=(k_hbm, v_hbm)[which],
            dst_ref=kv_scr.at[which, pl.ds(own - d * rows, rows)],
            send_sem=kv_send.at[which, d - 1],
            recv_sem=kv_recv.at[which, d - 1],
            device_id={"ctx": lax.rem(me + d, n_ctx)},
            device_id_type=MESH,
        )

    def halo_copy(which):
        src, dst = ((x_hbm, halo_x), (bc_hbm, halo_bc))[which]
        return pltpu.make_async_remote_copy(
            src_ref=src.at[src.shape[0] - dst.shape[0] : src.shape[0]],
            dst_ref=dst,
            send_sem=halo_send.at[which],
            recv_sem=halo_recv.at[which],
            device_id={"ctx": lax.rem(me + 1, n_ctx)},
            device_id_type=MESH,
        )

    def state_copy():
        return pltpu.make_async_remote_copy(
            src_ref=state_out,
            dst_ref=state_in,
            send_sem=st_send,
            recv_sem=st_recv,
            device_id={"ctx": lax.rem(me + 1, n_ctx)},
            device_id_type=MESH,
        )

    def attn_copy(r, j):
        part = pl.ds(r * ROWS, ROWS)
        columns = pl.ds(pl.multiple_of(j * PAIR, PAIR), PAIR)
        return pltpu.make_async_remote_copy(
            src_ref=attn_scr.at[part, columns],
            dst_ref=attn_out.at[0, part, columns],
            send_sem=at_send.at[r, j],
            recv_sem=at_recv.at[r, j],
            device_id={"pipe": following},
            device_id_type=MESH,
        )

    def mix_copy(r):
        part = pl.ds(r * ROWS, ROWS)
        return pltpu.make_async_remote_copy(
            src_ref=mix_scr.at[part],
            dst_ref=mix_out.at[0, part],
            send_sem=mx_send.at[r],
            recv_sem=mx_recv.at[r],
            device_id={"pipe": following},
            device_id_type=MESH,
        )

    row = lax.broadcasted_iota(jnp.int32, (rows, rows), 0)
    col = lax.broadcasted_iota(jnp.int32, (rows, rows), 1)

    pl.semaphore_wait(barrier, n_ctx + 1)

    for d in range(1, n_ctx):

        @pl.when(me + d < n_ctx)
        def _():
            kv_copy(d, 0).start()
            kv_copy(d, 1).start()

    for which in range(2):
        halo_copy(which).start()

    scale = 1.0 / math.sqrt(ADIM)
    tile_row = lax.broadcasted_iota(jnp.int32, (ROWS, ROWS), 0)
    tile_col = lax.broadcasted_iota(jnp.int32, (ROWS, ROWS), 1)

    def doc_tile(position):
        columns = pl.ds(pl.multiple_of(position, ROWS), ROWS)
        return jnp.broadcast_to(doc_ref[:, columns].astype(jnp.float32), (ROWS, ROWS))

    def make_mask(r, low):
        query_docs = doc_tile(me * rows + r * ROWS).T
        for c in range(low // ROWS, window // ROWS + 1):
            behind = window - c * ROWS
            position = me * rows + r * ROWS - behind
            allowed = doc_tile(jnp.maximum(position, 0)) == query_docs
            if behind == 0:
                allowed = allowed & (tile_row >= tile_col)
            elif behind == window:
                allowed = allowed & (tile_row < tile_col)
            if behind > r * ROWS:
                allowed = allowed & (tile_row * 0 + position >= 0)
            mask_scr[pl.ds(r * ROWS, ROWS), pl.ds(c * ROWS, ROWS)] = jnp.where(allowed, 0.0, -1e30)

    def attend(r, low):
        part = pl.ds(r * ROWS, ROWS)
        keys = pl.ds(own + r * ROWS - window + low, window + ROWS - low)

        def pair(j, carry):
            columns = pl.ds(pl.multiple_of(j * PAIR, PAIR), PAIR)
            query = q_ref[part, columns]
            query = jnp.concatenate([query[:, :ADIM], query[:, ADIM:]], axis=0)
            mask = mask_scr[part, low:]
            logits = nt(query, kv_scr[0, keys]) * scale + jnp.concatenate([mask, mask], axis=0)
            probs = jnp.exp(logits - jnp.max(logits, axis=1, keepdims=True))
            total = jnp.sum(probs, axis=1, keepdims=True)
            out = (mm(probs.astype(jnp.bfloat16), kv_scr[1, keys]) / total).astype(jnp.bfloat16)
            attn_scr[part, columns] = jnp.concatenate([out[:ROWS], out[ROWS:]], axis=1)
            attn_copy(r, j).start()
            return carry

        lax.fori_loop(0, pairs, pair, 0, unroll=True)

    loads[12].wait()
    if n_ctx == 2:

        @pl.when(me == 0)
        def _():
            loads[10].wait()
            loads[11].wait()
            for r in range(blocks):
                make_mask(r, window - r * ROWS)
                loads[queries_at + r].wait()
                attend(r, window - r * ROWS)

    @pl.when(me >= (1 if n_ctx == 2 else 0))
    def _():
        for r in range(blocks):
            make_mask(r, 0)
        loads[10].wait()
        loads[11].wait()
        for d in range(1, n_ctx):

            @pl.when(me - d >= 0)
            def _():
                kv_copy(d, 0).wait_recv()
                kv_copy(d, 1).wait_recv()

            if n_ctx > 2:

                @pl.when(me - d < 0)
                def _():
                    absent = pl.ds(own - d * rows, rows)
                    kv_scr[0, absent] = jnp.zeros((rows, ADIM), jnp.bfloat16)
                    kv_scr[1, absent] = jnp.zeros((rows, ADIM), jnp.bfloat16)

        for r in range(blocks):
            loads[queries_at + r].wait()
            attend(r, 0)

    count = step_ref.shape[0]
    e_row = lax.rem(lax.broadcasted_iota(jnp.int32, (3 * count, width), 0), count)
    e_col = lax.broadcasted_iota(jnp.int32, (3 * count, width), 1) // HDIM
    expand[...] = jnp.where(e_row == e_col, 1.0, 0.0).astype(jnp.bfloat16)

    for i in (0, 1, 3, 4, 5, 6, 7, 8):
        loads[i].wait()
    for which in range(2):
        halo_copy(which).wait_recv()
    keep = jnp.where(me > 0, 1.0, 0.0)
    x_ext[0:8] = halo_x[...].astype(jnp.float32)[HALO - 8 :] * keep
    x_ext[8 : 8 + rows] = x_ref[...].astype(jnp.float32)
    bc_ext[0:16] = halo_bc[...].astype(jnp.float32)[2 * HALO - 16 :] * keep
    bc_ext[16 : 16 + 2 * rows] = bc_ref[...].astype(jnp.float32)
    first = 8 - (KERNEL - 1)

    def bc_conv(which):
        total = jnp.zeros((rows, STATE), jnp.float32)
        for tap in range(KERNEL):
            tokens = bc_ext[pl.ds(2 * (first + tap) + which, rows, stride=2)]
            total = total + cbw_ref[tap, which : which + 1] * tokens
        return silu(total)

    b_conv = bc_conv(0)
    c_conv = bc_conv(1)
    gram = jnp.where(row >= col, nt(c_conv, b_conv, highest), 0.0)
    high, low = split2(gram)
    g_hi[...] = high
    g_lo[...] = low
    bt_hi, bt_lo = split2(b_conv.T)
    c_hi, c_lo = split2(c_conv)

    raw = step_ref[...].astype(jnp.float32).T + bias_ref[...]
    step = jnp.maximum(raw, 0.0) + jnp.log1p(jnp.exp(-jnp.abs(raw)))
    log_decay = -rate_ref[...] * step
    lower = jnp.where(row >= col, 1.0, 0.0)
    cumulative = jnp.dot(lower, log_decay, precision=highest, preferred_element_type=jnp.float32)
    grow = split3(jnp.exp(-cumulative) * step)
    fall = split3(jnp.exp(cumulative))
    skip = split3(jnp.broadcast_to(skip_ref[...], (8, count)))

    def prepare(j, carry):
        lanes = pl.ds(pl.multiple_of(j * LANES, LANES), LANES)
        total = cw_ref[0:1, lanes] * x_ext[first : first + rows, lanes]
        for tap in range(1, KERNEL):
            total = total + cw_ref[tap : tap + 1, lanes] * x_ext[first + tap : first + tap + rows, lanes]
        conv = silu(total)
        xc_scr[:, lanes] = conv
        high, low = split2(conv * mm(grow, expand[:, lanes]))
        xt_hi[:, lanes] = high
        xt_lo[:, lanes] = low
        state_acc[:, lanes] = mm(bt_hi, high) + mm(bt_hi, low) + mm(bt_lo, high)
        return carry

    lax.fori_loop(0, width // LANES, prepare, 0)

    @pl.when(me == 0)
    def _():
        state_in[...] = jnp.zeros_like(state_in)

    if n_ctx > 1:

        @pl.when(me > 0)
        def _():
            state_copy().wait_recv()

        @pl.when(me < n_ctx - 1)
        def _():
            end = mm(fall[rows - 16 :], expand[...])[15:16]
            state_out[...] = (end * (state_in[...].astype(jnp.float32) + state_acc[...])).astype(
                jnp.bfloat16
            )
            state_copy().start()

    loads[2].wait()
    loads[9].wait()
    for r in range(blocks):
        part = slice(r * ROWS, (r + 1) * ROWS)
        upto = (r + 1) * ROWS

        def mix_lanes(j, square):
            lanes = pl.ds(pl.multiple_of(j * LANES, LANES), LANES)
            inside = mm(g_hi[part, :upto], xt_hi[:upto, lanes])
            inside = inside + mm(g_hi[part, :upto], xt_lo[:upto, lanes])
            inside = inside + mm(g_lo[part, :upto], xt_hi[:upto, lanes])
            carried = state_in[:, lanes]
            inside = inside + mm(c_hi[part], carried) + mm(c_lo[part], carried)
            e_part = expand[:, lanes]
            out = inside * mm(fall[part], e_part) + mm(skip, e_part)[0:1] * xc_scr[part, lanes]
            out = out * silu(z_ref[part, lanes].astype(jnp.float32))
            gated[:, lanes] = out
            return square + jnp.sum(out * out, axis=1, keepdims=True)

        square = lax.fori_loop(0, width // LANES, mix_lanes, jnp.zeros((ROWS, 1), jnp.float32))
        norm = lax.rsqrt(square * (1.0 / width) + 1e-05)
        mix_scr[part] = (gated[...] * norm * gain_ref[...]).astype(jnp.bfloat16)
        mix_copy(r).start()

    for d in range(1, n_ctx):

        @pl.when(me + d < n_ctx)
        def _():
            kv_copy(d, 0).wait_send()
            kv_copy(d, 1).wait_send()

    for which in range(2):
        halo_copy(which).wait_send()
    if n_ctx > 1:

        @pl.when(me < n_ctx - 1)
        def _():
            state_copy().wait_send()

    for r in range(blocks):
        for j in range(pairs):
            attn_copy(r, j).wait()
    for r in range(blocks):
        mix_copy(r).wait()


def store(mix_ref, attn_ref, mix_out, attn_out, sem):
    copies = [
        pltpu.make_async_copy(source, target, sem.at[i])
        for i, (source, target) in enumerate(((mix_ref, mix_out), (attn_ref, attn_out)))
    ]
    for copy in copies:
        copy.start()
    for copy in copies:
        copy.wait()


def local(
    mamba_input,
    mamba_bc,
    gate_input,
    step_input,
    step_bias,
    decay_rate,
    skip_gain,
    conv_weight,
    conv_bc_weight,
    norm_gain,
    queries,
    attn_keys,
    attn_values,
    documents,
):
    n_ctx = lax.axis_size("ctx")
    n_pipe = lax.axis_size("pipe")
    _, rows, width = mamba_input.shape
    q_width = queries.shape[2]
    pairs = q_width // PAIR
    blocks = rows // ROWS
    count = step_input.shape[2]
    bf16, f32 = jnp.bfloat16, jnp.float32
    others = max(n_ctx - 1, 1)
    dma = pltpu.SemaphoreType.DMA
    operands = (
        mamba_input[0],
        mamba_bc[0].reshape(2 * rows, STATE),
        gate_input[0],
        step_input[0].T,
        step_bias,
        decay_rate,
        skip_gain,
        conv_weight[0],
        conv_bc_weight[0],
        norm_gain,
        queries[0],
        attn_keys[0],
        attn_values[0],
        documents,
    )
    mixer, attended = pl.pallas_call(
        functools.partial(kernel, n_ctx, n_pipe),
        out_shape=(pltpu.VMEM(mamba_input.shape, bf16), pltpu.VMEM(queries.shape, bf16)),
        in_specs=[pl.BlockSpec(memory_space=pltpu.HBM)] * len(operands),
        out_specs=[pl.BlockSpec(memory_space=pltpu.VMEM)] * 2,
        scratch_shapes=[
            pltpu.VMEM(operand.shape, operand.dtype)
            for operand in operands[:11] + operands[13:]
        ]
        + [
            dma((13 + blocks,)),
            pltpu.VMEM((2, n_ctx * rows, ADIM), bf16),
            pltpu.VMEM((HALO, width), bf16),
            pltpu.VMEM((2 * HALO, STATE), bf16),
            pltpu.VMEM((STATE, width), bf16),
            pltpu.VMEM((STATE, width), bf16),
            pltpu.VMEM((rows, q_width), bf16),
            pltpu.VMEM((rows, width), bf16),
            pltpu.VMEM((rows, documents.shape[1] // 2 + ROWS), f32),
            pltpu.VMEM((3 * count, width), bf16),
            pltpu.VMEM((rows + 8, width), f32),
            pltpu.VMEM((2 * rows + 16, STATE), f32),
            pltpu.VMEM((rows, width), f32),
            pltpu.VMEM((rows, width), bf16),
            pltpu.VMEM((rows, width), bf16),
            pltpu.VMEM((rows, rows), bf16),
            pltpu.VMEM((rows, rows), bf16),
            pltpu.VMEM((STATE, width), f32),
            pltpu.VMEM((ROWS, width), f32),
            dma((2, others)),
            dma((2, others)),
            dma((2,)),
            dma((2,)),
            dma,
            dma,
            dma((blocks, pairs)),
            dma((blocks, pairs)),
            dma((blocks,)),
            dma((blocks,)),
        ],
        compiler_params=pltpu.CompilerParams(
            collective_id=0, has_side_effects=True, vmem_limit_bytes=50_000_000
        ),
    )(*[pltpu.with_memory_space_constraint(operand, pltpu.HBM) for operand in operands])
    return pl.pallas_call(
        store,
        out_shape=(
            jax.ShapeDtypeStruct(mamba_input.shape, bf16),
            jax.ShapeDtypeStruct(queries.shape, bf16),
        ),
        in_specs=[pl.BlockSpec(memory_space=pltpu.VMEM)] * 2,
        out_specs=[pl.BlockSpec(memory_space=pltpu.HBM)] * 2,
        scratch_shapes=[dma((2,))],
        compiler_params=pltpu.CompilerParams(vmem_limit_bytes=50_000_000),
    )(mixer, attended)


def solution(mesh):
    in_specs = (
        P("pipe", "ctx", "tp"),
        P("pipe", "ctx", None, "tp"),
        P("pipe", "ctx", "tp"),
        P("pipe", "ctx", "tp"),
        P("pipe", "tp"),
        P("pipe", "tp"),
        P("pipe", "tp"),
        P("pipe", None, "tp"),
        P("pipe", None, None, "tp"),
        P("pipe", "tp"),
        P("pipe", "ctx", "tp"),
        P("pipe", "ctx", "tp"),
        P("pipe", "ctx", "tp"),
        P("pipe", None),
    )
    out_specs = (P("pipe", "ctx", "tp"), P("pipe", "ctx", "tp"))
    return jax.shard_map(local, mesh=mesh, in_specs=in_specs, out_specs=out_specs, check_vma=False)
```

```python
import functools
import math

import jax
import jax.numpy as jnp
from jax import lax
from jax.experimental import pallas as pl
from jax.experimental.pallas import tpu as pltpu
from jax.sharding import PartitionSpec as P

HDIM = 64
STATE = 128
KERNEL = 4
ADIM = 128
HALO = 16
LANES = 256
ROWS = 128
PAIR = 2 * ADIM
MESH = pl.DeviceIdType.MESH
highest = lax.Precision.HIGHEST


def silu(v):
    half = 0.5 * v
    return half + half * jnp.tanh(half)


def split2(v):
    high = v.astype(jnp.bfloat16)
    return high, (v - high.astype(jnp.float32)).astype(jnp.bfloat16)


def split3(v):
    high = v.astype(jnp.bfloat16)
    rest = v - high.astype(jnp.float32)
    mid = rest.astype(jnp.bfloat16)
    low = (rest - mid.astype(jnp.float32)).astype(jnp.bfloat16)
    return jnp.concatenate([high, mid, low], axis=1)


def mm(a, b):
    return jnp.dot(a, b, preferred_element_type=jnp.float32)


def nt(a, b, precision=None):
    return lax.dot_general(
        a, b, (((1,), (1,)), ((), ())), precision=precision, preferred_element_type=jnp.float32
    )


def kernel(
    n_ctx,
    n_pipe,
    x_hbm,
    bc_hbm,
    z_hbm,
    step_hbm,
    bias_hbm,
    rate_hbm,
    skip_hbm,
    cw_hbm,
    cbw_hbm,
    gain_hbm,
    q_hbm,
    k_hbm,
    v_hbm,
    doc_hbm,
    received,
    x_ref,
    bc_ref,
    z_ref,
    step_ref,
    bias_ref,
    rate_ref,
    skip_ref,
    cw_ref,
    cbw_ref,
    gain_ref,
    q_ref,
    doc_ref,
    load_sem,
    kv_scr,
    halo_x,
    halo_bc,
    state_in,
    state_out,
    attn_scr,
    mix_scr,
    mask_scr,
    expand,
    x_ext,
    bc_ext,
    xc_scr,
    xt_hi,
    xt_lo,
    g_hi,
    g_lo,
    state_acc,
    gated,
    kv_send,
    kv_recv,
    halo_send,
    halo_recv,
    st_send,
    st_recv,
    tri_out,
    tri_in,
    diag_out,
    diag_in,
    first_values,
    at_send,
    at_recv,
    tri_send,
    tri_recv,
    mx_send,
    mx_recv,
):
    me = lax.axis_index("ctx")
    stage = lax.axis_index("pipe")
    following = lax.rem(stage + 1, n_pipe)
    previous = lax.rem(stage + n_pipe - 1, n_pipe)
    rows, width = x_ref.shape
    pairs = q_ref.shape[1] // PAIR
    blocks = rows // ROWS
    window = doc_ref.shape[1] // 2
    own = (n_ctx - 1) * rows

    local_keys = pl.ds(own, rows)
    sources = (x_hbm, bc_hbm, z_hbm, step_hbm, bias_hbm, rate_hbm, skip_hbm)
    sources += (cw_hbm, cbw_hbm, gain_hbm, k_hbm, v_hbm, doc_hbm)
    targets = (x_ref, bc_ref, z_ref, step_ref, bias_ref, rate_ref, skip_ref, cw_ref, cbw_ref, gain_ref)
    targets += (kv_scr.at[0, local_keys], kv_scr.at[1, local_keys], doc_ref)
    for r in range(blocks):
        part = pl.ds(r * ROWS, ROWS)
        sources += (q_hbm.at[part],)
        targets += (q_ref.at[part],)
    loads = [
        pltpu.make_async_copy(source, target, load_sem.at[i])
        for i, (source, target) in enumerate(zip(sources, targets))
    ]
    queries_at = 13
    order = (*range(1, blocks), 0)
    for i in (12, 10, 11, *(queries_at + r for r in order), 0, 1, 3, 4, 5, 6, 7, 8, 9, 2):
        loads[i].start()

    barrier = pltpu.get_barrier_semaphore()
    pl.semaphore_signal(barrier, inc=1, device_id={"pipe": following}, device_id_type=MESH)
    pl.semaphore_signal(barrier, inc=1, device_id={"pipe": previous}, device_id_type=MESH)
    for d in range(1, n_ctx):
        pl.semaphore_signal(
            barrier, inc=1, device_id={"ctx": lax.rem(me + d, n_ctx)}, device_id_type=MESH
        )
    def kv_copy(d, which):
        return pltpu.make_async_remote_copy(
            src_ref=(k_hbm, v_hbm)[which],
            dst_ref=kv_scr.at[which, pl.ds(own - d * rows, rows)],
            send_sem=kv_send.at[which, d - 1],
            recv_sem=kv_recv.at[which, d - 1],
            device_id={"ctx": lax.rem(me + d, n_ctx)},
            device_id_type=MESH,
        )

    def halo_copy(which):
        src, dst = ((x_hbm, halo_x), (bc_hbm, halo_bc))[which]
        return pltpu.make_async_remote_copy(
            src_ref=src.at[src.shape[0] - dst.shape[0] : src.shape[0]],
            dst_ref=dst,
            send_sem=halo_send.at[which],
            recv_sem=halo_recv.at[which],
            device_id={"ctx": lax.rem(me + 1, n_ctx)},
            device_id_type=MESH,
        )

    def state_copy():
        return pltpu.make_async_remote_copy(
            src_ref=state_out,
            dst_ref=state_in,
            send_sem=st_send,
            recv_sem=st_recv,
            device_id={"ctx": lax.rem(me + 1, n_ctx)},
            device_id_type=MESH,
        )

    def attn_copy(r, j):
        part = pl.ds(r * ROWS, ROWS)
        columns = pl.ds(pl.multiple_of(j * PAIR, PAIR), PAIR)
        return pltpu.make_async_remote_copy(
            src_ref=attn_scr.at[part, columns],
            dst_ref=received.at[part, pl.ds(pl.multiple_of(width + j * PAIR, PAIR), PAIR)],
            send_sem=at_send.at[r, j],
            recv_sem=at_recv.at[r, j],
            device_id={"pipe": following},
            device_id_type=MESH,
        )

    def first_copy(i):
        if i < pairs:
            src, dst = tri_out.at[i], tri_in.at[i]
        elif i == pairs:
            src, dst = diag_out, diag_in
        else:
            src, dst = v_hbm.at[pl.ds(0, ROWS)], first_values
        return pltpu.make_async_remote_copy(
            src_ref=src,
            dst_ref=dst,
            send_sem=tri_send.at[i],
            recv_sem=tri_recv.at[i],
            device_id={"pipe": following},
            device_id_type=MESH,
        )

    def mix_copy(r):
        part = pl.ds(r * ROWS, ROWS)
        return pltpu.make_async_remote_copy(
            src_ref=mix_scr.at[part],
            dst_ref=received.at[part, pl.ds(0, width)],
            send_sem=mx_send.at[r],
            recv_sem=mx_recv.at[r],
            device_id={"pipe": following},
            device_id_type=MESH,
        )

    row = lax.broadcasted_iota(jnp.int32, (rows, rows), 0)
    col = lax.broadcasted_iota(jnp.int32, (rows, rows), 1)

    pl.semaphore_wait(barrier, n_ctx + 1)

    for d in range(1, n_ctx):

        @pl.when(me + d < n_ctx)
        def _():
            kv_copy(d, 0).start()
            kv_copy(d, 1).start()

    @pl.when(me == 0)
    def _():
        first_copy(pairs + 1).start()

    for which in range(2):
        halo_copy(which).start()

    scale = 1.0 / math.sqrt(ADIM)
    tile_row = lax.broadcasted_iota(jnp.int32, (ROWS, ROWS), 0)
    tile_col = lax.broadcasted_iota(jnp.int32, (ROWS, ROWS), 1)

    def doc_tile(position):
        columns = pl.ds(pl.multiple_of(position, ROWS), ROWS)
        return jnp.broadcast_to(doc_ref[:, columns].astype(jnp.float32), (ROWS, ROWS))

    def make_mask(r, low):
        query_docs = doc_tile(me * rows + r * ROWS).T
        for c in range(low // ROWS, window // ROWS + 1):
            behind = window - c * ROWS
            position = me * rows + r * ROWS - behind
            allowed = doc_tile(jnp.maximum(position, 0)) == query_docs
            if behind == 0:
                allowed = allowed & (tile_row >= tile_col)
            elif behind == window:
                allowed = allowed & (tile_row < tile_col)
            if behind > r * ROWS:
                allowed = allowed & (tile_row * 0 + position >= 0)
            mask_scr[pl.ds(r * ROWS, ROWS), pl.ds(c * ROWS, ROWS)] = jnp.where(allowed, 0.0, -1e30)

    def attend(r, low):
        part = pl.ds(r * ROWS, ROWS)
        keys = pl.ds(own + r * ROWS - window + low, window + ROWS - low)

        def pair(j, carry):
            columns = pl.ds(pl.multiple_of(j * PAIR, PAIR), PAIR)
            query = q_ref[part, columns]
            query = jnp.concatenate([query[:, :ADIM], query[:, ADIM:]], axis=0)
            mask = mask_scr[part, low:]
            logits = nt(query, kv_scr[0, keys]) * scale + jnp.concatenate([mask, mask], axis=0)
            probs = jnp.exp(logits - jnp.max(logits, axis=1, keepdims=True))
            total = jnp.sum(probs, axis=1, keepdims=True)
            out = (mm(probs.astype(jnp.bfloat16), kv_scr[1, keys]) / total).astype(jnp.bfloat16)
            attn_scr[part, columns] = jnp.concatenate([out[:ROWS], out[ROWS:]], axis=1)
            attn_copy(r, j).start()
            return carry

        lax.fori_loop(0, pairs, pair, 0, unroll=True)

    def send_first():
        part = pl.ds(0, ROWS)
        keys = pl.ds(own, ROWS)
        diagonals = []
        for j in range(pairs):
            query = q_ref[part, j * PAIR : (j + 1) * PAIR]
            query = jnp.concatenate([query[:, :ADIM], query[:, ADIM:]], axis=0)
            mask = mask_scr[part, pl.ds(window, ROWS)]
            logits = nt(query, kv_scr[0, keys]) * scale + jnp.concatenate([mask, mask], axis=0)
            probs = jnp.exp(logits - jnp.max(logits, axis=1, keepdims=True))
            probs = probs / jnp.sum(probs, axis=1, keepdims=True)
            second = probs[ROWS:]
            square = jnp.where(tile_row >= tile_col, probs[:ROWS], second.T)
            tri_out[j] = square.astype(jnp.bfloat16)
            first_copy(j).start()
            diagonals.append(
                jnp.sum(jnp.where(tile_row == tile_col, second, 0.0), axis=0, keepdims=True)
            )
        spare = diag_out.shape[0] - pairs
        if spare:
            diagonals.append(jnp.zeros((spare, ROWS), jnp.float32))
        diag_out[...] = jnp.concatenate(diagonals, axis=0)
        first_copy(pairs).start()

    def receive_first():
        for i in range(pairs + 2):
            first_copy(i).wait_recv()
        values = first_values[...]
        for j in range(pairs):
            square = tri_in[j].astype(jnp.float32)
            diagonal = jnp.where(tile_row == tile_col, diag_in[j : j + 1], 0.0)
            one = jnp.where(tile_row >= tile_col, square, 0.0).astype(jnp.bfloat16)
            two = jnp.where(tile_row < tile_col, square, diagonal).T.astype(jnp.bfloat16)
            both = jnp.concatenate([mm(one, values), mm(two, values)], axis=1)
            received[0:ROWS, width + j * PAIR : width + (j + 1) * PAIR] = both.astype(jnp.bfloat16)

    count = step_ref.shape[0]
    e_row = lax.rem(lax.broadcasted_iota(jnp.int32, (3 * count, width), 0), count)
    e_col = lax.broadcasted_iota(jnp.int32, (3 * count, width), 1) // HDIM
    expand[...] = jnp.where(e_row == e_col, 1.0, 0.0).astype(jnp.bfloat16)

    loads[12].wait()

    @pl.when(me == 0)
    def _():
        loads[10].wait()
        loads[11].wait()
        for r in order:
            make_mask(r, window - r * ROWS)
            loads[queries_at + r].wait()
            if r > 0:
                attend(r, window - r * ROWS)
            else:
                send_first()

    @pl.when(me > 0)
    def _():
        for r in range(blocks):
            make_mask(r, 0)
        loads[10].wait()
        loads[11].wait()
        for d in range(1, n_ctx):

            @pl.when(me - d >= 0)
            def _():
                kv_copy(d, 0).wait_recv()
                kv_copy(d, 1).wait_recv()

            if n_ctx > 2:

                @pl.when(me - d < 0)
                def _():
                    absent = pl.ds(own - d * rows, rows)
                    kv_scr[0, absent] = jnp.zeros((rows, ADIM), jnp.bfloat16)
                    kv_scr[1, absent] = jnp.zeros((rows, ADIM), jnp.bfloat16)

        for r in order:
            loads[queries_at + r].wait()
            attend(r, 0)

    for i in (0, 1, 3, 4, 5, 6, 7, 8):
        loads[i].wait()
    for which in range(2):
        halo_copy(which).wait_recv()
    keep = jnp.where(me > 0, 1.0, 0.0)
    x_ext[0:8] = halo_x[...].astype(jnp.float32)[HALO - 8 :] * keep
    x_ext[8 : 8 + rows] = x_ref[...].astype(jnp.float32)
    bc_ext[0:16] = halo_bc[...].astype(jnp.float32)[2 * HALO - 16 :] * keep
    bc_ext[16 : 16 + 2 * rows] = bc_ref[...].astype(jnp.float32)
    first = 8 - (KERNEL - 1)

    def bc_conv(which):
        total = jnp.zeros((rows, STATE), jnp.float32)
        for tap in range(KERNEL):
            tokens = bc_ext[pl.ds(2 * (first + tap) + which, rows, stride=2)]
            total = total + cbw_ref[tap, which : which + 1] * tokens
        return silu(total)

    b_conv = bc_conv(0)
    c_conv = bc_conv(1)
    gram = jnp.where(row >= col, nt(c_conv, b_conv, highest), 0.0)
    high, low = split2(gram)
    g_hi[...] = high
    g_lo[...] = low
    bt_hi, bt_lo = split2(b_conv.T)
    c_hi, c_lo = split2(c_conv)

    raw = step_ref[...].astype(jnp.float32).T + bias_ref[...]
    step = jnp.maximum(raw, 0.0) + jnp.log1p(jnp.exp(-jnp.abs(raw)))
    log_decay = -rate_ref[...] * step
    lower = jnp.where(row >= col, 1.0, 0.0)
    cumulative = jnp.dot(lower, log_decay, precision=highest, preferred_element_type=jnp.float32)
    grow = split3(jnp.exp(-cumulative) * step)
    fall = split3(jnp.exp(cumulative))
    skip = split3(jnp.broadcast_to(skip_ref[...], (8, count)))

    def prepare(j, carry):
        lanes = pl.ds(pl.multiple_of(j * LANES, LANES), LANES)
        total = cw_ref[0:1, lanes] * x_ext[first : first + rows, lanes]
        for tap in range(1, KERNEL):
            total = total + cw_ref[tap : tap + 1, lanes] * x_ext[first + tap : first + tap + rows, lanes]
        conv = silu(total)
        xc_scr[:, lanes] = conv
        high, low = split2(conv * mm(grow, expand[:, lanes]))
        xt_hi[:, lanes] = high
        xt_lo[:, lanes] = low
        state_acc[:, lanes] = mm(bt_hi, high) + mm(bt_hi, low) + mm(bt_lo, high)
        return carry

    lax.fori_loop(0, width // LANES, prepare, 0, unroll=4)

    @pl.when(me == 0)
    def _():
        state_in[...] = jnp.zeros_like(state_in)

    if n_ctx > 1:

        @pl.when(me > 0)
        def _():
            state_copy().wait_recv()

        @pl.when(me < n_ctx - 1)
        def _():
            end = mm(fall[rows - 16 :], expand[...])[15:16]
            state_out[...] = (end * (state_in[...].astype(jnp.float32) + state_acc[...])).astype(
                jnp.bfloat16
            )
            state_copy().start()

    loads[2].wait()
    loads[9].wait()
    for r in range(blocks):
        part = slice(r * ROWS, (r + 1) * ROWS)
        upto = (r + 1) * ROWS

        def mix_lanes(j, square):
            lanes = pl.ds(pl.multiple_of(j * LANES, LANES), LANES)
            inside = mm(g_hi[part, :upto], xt_hi[:upto, lanes])
            inside = inside + mm(g_hi[part, :upto], xt_lo[:upto, lanes])
            inside = inside + mm(g_lo[part, :upto], xt_hi[:upto, lanes])
            carried = state_in[:, lanes]
            inside = inside + mm(c_hi[part], carried) + mm(c_lo[part], carried)
            e_part = expand[:, lanes]
            out = inside * mm(fall[part], e_part) + mm(skip, e_part)[0:1] * xc_scr[part, lanes]
            out = out * silu(z_ref[part, lanes].astype(jnp.float32))
            gated[:, lanes] = out
            return square + jnp.sum(out * out, axis=1, keepdims=True)

        square = lax.fori_loop(
            0, width // LANES, mix_lanes, jnp.zeros((ROWS, 1), jnp.float32), unroll=4
        )
        norm = lax.rsqrt(square * (1.0 / width) + 1e-05)
        mix_scr[part] = (gated[...] * norm * gain_ref[...]).astype(jnp.bfloat16)
        mix_copy(r).start()

    for d in range(1, n_ctx):

        @pl.when(me + d < n_ctx)
        def _():
            kv_copy(d, 0).wait_send()
            kv_copy(d, 1).wait_send()

    for which in range(2):
        halo_copy(which).wait_send()
    if n_ctx > 1:

        @pl.when(me < n_ctx - 1)
        def _():
            state_copy().wait_send()

    @pl.when(me == 0)
    def _():
        receive_first()
        for i in range(pairs + 2):
            first_copy(i).wait_send()

    @pl.when(me > 0)
    def _():
        for j in range(pairs):
            attn_copy(0, j).wait()

    for r in range(1, blocks):
        for j in range(pairs):
            attn_copy(r, j).wait()
    for r in range(blocks):
        mix_copy(r).wait()


def store(received, mix_out, attn_out, sem):
    width = mix_out.shape[2]
    copies = [
        pltpu.make_async_copy(received.at[:, pl.ds(0, width)], mix_out.at[0], sem.at[0]),
        pltpu.make_async_copy(
            received.at[:, pl.ds(width, attn_out.shape[2])], attn_out.at[0], sem.at[1]
        ),
    ]
    for copy in copies:
        copy.start()
    for copy in copies:
        copy.wait()


def local(
    mamba_input,
    mamba_bc,
    gate_input,
    step_input,
    step_bias,
    decay_rate,
    skip_gain,
    conv_weight,
    conv_bc_weight,
    norm_gain,
    queries,
    attn_keys,
    attn_values,
    documents,
):
    n_ctx = lax.axis_size("ctx")
    n_pipe = lax.axis_size("pipe")
    _, rows, width = mamba_input.shape
    q_width = queries.shape[2]
    pairs = q_width // PAIR
    blocks = rows // ROWS
    count = step_input.shape[2]
    bf16, f32 = jnp.bfloat16, jnp.float32
    others = max(n_ctx - 1, 1)
    dma = pltpu.SemaphoreType.DMA
    operands = (
        mamba_input[0],
        mamba_bc[0].reshape(2 * rows, STATE),
        gate_input[0],
        step_input[0].T,
        step_bias,
        decay_rate,
        skip_gain,
        conv_weight[0],
        conv_bc_weight[0],
        norm_gain,
        queries[0],
        attn_keys[0],
        attn_values[0],
        documents,
    )
    received = pl.pallas_call(
        functools.partial(kernel, n_ctx, n_pipe),
        out_shape=pltpu.VMEM((rows, width + q_width), bf16),
        in_specs=[pl.BlockSpec(memory_space=pltpu.HBM)] * len(operands),
        out_specs=pl.BlockSpec(memory_space=pltpu.VMEM),
        scratch_shapes=[
            pltpu.VMEM(operand.shape, operand.dtype)
            for operand in operands[:11] + operands[13:]
        ]
        + [
            dma((13 + blocks,)),
            pltpu.VMEM((2, n_ctx * rows, ADIM), bf16),
            pltpu.VMEM((HALO, width), bf16),
            pltpu.VMEM((2 * HALO, STATE), bf16),
            pltpu.VMEM((STATE, width), bf16),
            pltpu.VMEM((STATE, width), bf16),
            pltpu.VMEM((rows, q_width), bf16),
            pltpu.VMEM((rows, width), bf16),
            pltpu.VMEM((rows, documents.shape[1] // 2 + ROWS), f32),
            pltpu.VMEM((3 * count, width), bf16),
            pltpu.VMEM((rows + 8, width), f32),
            pltpu.VMEM((2 * rows + 16, STATE), f32),
            pltpu.VMEM((rows, width), f32),
            pltpu.VMEM((rows, width), bf16),
            pltpu.VMEM((rows, width), bf16),
            pltpu.VMEM((rows, rows), bf16),
            pltpu.VMEM((rows, rows), bf16),
            pltpu.VMEM((STATE, width), f32),
            pltpu.VMEM((ROWS, width), f32),
            dma((2, others)),
            dma((2, others)),
            dma((2,)),
            dma((2,)),
            dma,
            dma,
            pltpu.VMEM((pairs, ROWS, ROWS), bf16),
            pltpu.VMEM((pairs, ROWS, ROWS), bf16),
            pltpu.VMEM((-(-pairs // 8) * 8, ROWS), f32),
            pltpu.VMEM((-(-pairs // 8) * 8, ROWS), f32),
            pltpu.VMEM((ROWS, ADIM), bf16),
            dma((blocks, pairs)),
            dma((blocks, pairs)),
            dma((pairs + 2,)),
            dma((pairs + 2,)),
            dma((blocks,)),
            dma((blocks,)),
        ],
        compiler_params=pltpu.CompilerParams(
            collective_id=0, has_side_effects=True, vmem_limit_bytes=50_000_000
        ),
    )(*[pltpu.with_memory_space_constraint(operand, pltpu.HBM) for operand in operands])
    return pl.pallas_call(
        store,
        out_shape=(
            jax.ShapeDtypeStruct(mamba_input.shape, bf16),
            jax.ShapeDtypeStruct(queries.shape, bf16),
        ),
        in_specs=[pl.BlockSpec(memory_space=pltpu.VMEM)],
        out_specs=[pl.BlockSpec(memory_space=pltpu.HBM)] * 2,
        scratch_shapes=[dma((2,))],
        compiler_params=pltpu.CompilerParams(vmem_limit_bytes=50_000_000),
    )(received)


def solution(mesh):
    in_specs = (
        P("pipe", "ctx", "tp"),
        P("pipe", "ctx", None, "tp"),
        P("pipe", "ctx", "tp"),
        P("pipe", "ctx", "tp"),
        P("pipe", "tp"),
        P("pipe", "tp"),
        P("pipe", "tp"),
        P("pipe", None, "tp"),
        P("pipe", None, None, "tp"),
        P("pipe", "tp"),
        P("pipe", "ctx", "tp"),
        P("pipe", "ctx", "tp"),
        P("pipe", "ctx", "tp"),
        P("pipe", None),
    )
    out_specs = (P("pipe", "ctx", "tp"), P("pipe", "ctx", "tp"))
    return jax.shard_map(local, mesh=mesh, in_specs=in_specs, out_specs=out_specs, check_vma=False)
```

```python
import functools
import math

import jax
import jax.numpy as jnp
from jax import lax
from jax.experimental import pallas as pl
from jax.experimental.pallas import tpu as pltpu
from jax.sharding import PartitionSpec as P

HDIM = 64
STATE = 128
KERNEL = 4
ADIM = 128
HALO = 16
LANES = 256
ROWS = 128
PAIR = 2 * ADIM
MESH = pl.DeviceIdType.MESH
highest = lax.Precision.HIGHEST


def silu(v):
    half = 0.5 * v
    return half + half * jnp.tanh(half)


def split2(v):
    high = v.astype(jnp.bfloat16)
    return high, (v - high.astype(jnp.float32)).astype(jnp.bfloat16)


def split3(v):
    high = v.astype(jnp.bfloat16)
    rest = v - high.astype(jnp.float32)
    mid = rest.astype(jnp.bfloat16)
    low = (rest - mid.astype(jnp.float32)).astype(jnp.bfloat16)
    return jnp.concatenate([high, mid, low], axis=1)


def mm(a, b):
    return jnp.dot(a, b, preferred_element_type=jnp.float32)


def nt(a, b, precision=None):
    return lax.dot_general(
        a, b, (((1,), (1,)), ((), ())), precision=precision, preferred_element_type=jnp.float32
    )


def kernel(
    n_ctx,
    n_pipe,
    x_hbm,
    bc_hbm,
    z_hbm,
    step_hbm,
    bias_hbm,
    rate_hbm,
    skip_hbm,
    cw_hbm,
    cbw_hbm,
    gain_hbm,
    q_hbm,
    k_hbm,
    v_hbm,
    doc_hbm,
    received,
    x_ref,
    bc_ref,
    z_ref,
    step_ref,
    bias_ref,
    rate_ref,
    skip_ref,
    cw_ref,
    cbw_ref,
    gain_ref,
    q_ref,
    doc_ref,
    load_sem,
    kv_scr,
    halo_x,
    halo_bc,
    state_in,
    state_out,
    attn_scr,
    mix_scr,
    mask_scr,
    expand,
    x_ext,
    bc_ext,
    xc_scr,
    xt_hi,
    xt_lo,
    g_hi,
    g_lo,
    state_acc,
    gated,
    kv_send,
    kv_recv,
    halo_send,
    halo_recv,
    st_send,
    st_recv,
    tri_out,
    tri_in,
    diag_out,
    diag_in,
    first_values,
    at_send,
    at_recv,
    tri_send,
    tri_recv,
    mx_send,
    mx_recv,
):
    me = lax.axis_index("ctx")
    stage = lax.axis_index("pipe")
    following = lax.rem(stage + 1, n_pipe)
    previous = lax.rem(stage + n_pipe - 1, n_pipe)
    rows, width = x_ref.shape
    pairs = q_ref.shape[1] // PAIR
    blocks = rows // ROWS
    window = doc_ref.shape[1] // 2
    own = (n_ctx - 1) * rows

    local_keys = pl.ds(own, rows)
    sources = (x_hbm, bc_hbm, z_hbm, step_hbm, bias_hbm, rate_hbm, skip_hbm)
    sources += (cw_hbm, cbw_hbm, gain_hbm, k_hbm, v_hbm, doc_hbm)
    targets = (x_ref, bc_ref, z_ref, step_ref, bias_ref, rate_ref, skip_ref, cw_ref, cbw_ref, gain_ref)
    targets += (kv_scr.at[0, local_keys], kv_scr.at[1, local_keys], doc_ref)
    for r in range(blocks):
        part = pl.ds(r * ROWS, ROWS)
        sources += (q_hbm.at[part],)
        targets += (q_ref.at[part],)
    queries_at = 13
    order = (*range(1, blocks), 0)
    early = (12, 10, queries_at + order[0], 11)
    late = (*(queries_at + r for r in order[1:]), 0, 1, 3, 4, 5, 6, 7, 8, 9, 2)
    slot = {i: k for k, i in enumerate(early)} | {i: k for k, i in enumerate(late)}
    loads = [
        pltpu.make_async_copy(source, target, load_sem.at[slot[i]])
        for i, (source, target) in enumerate(zip(sources, targets))
    ]
    for i in early:
        loads[i].start()

    barrier = pltpu.get_barrier_semaphore()
    pl.semaphore_signal(barrier, inc=1, device_id={"pipe": following}, device_id_type=MESH)
    pl.semaphore_signal(barrier, inc=1, device_id={"pipe": previous}, device_id_type=MESH)
    for d in range(1, n_ctx):
        pl.semaphore_signal(
            barrier, inc=1, device_id={"ctx": lax.rem(me + d, n_ctx)}, device_id_type=MESH
        )
    def kv_copy(d, which):
        return pltpu.make_async_remote_copy(
            src_ref=(k_hbm, v_hbm)[which],
            dst_ref=kv_scr.at[which, pl.ds(own - d * rows, rows)],
            send_sem=kv_send.at[which, d - 1],
            recv_sem=kv_recv.at[which, d - 1],
            device_id={"ctx": lax.rem(me + d, n_ctx)},
            device_id_type=MESH,
        )

    def halo_copy(which):
        src, dst = ((x_hbm, halo_x), (bc_hbm, halo_bc))[which]
        return pltpu.make_async_remote_copy(
            src_ref=src.at[src.shape[0] - dst.shape[0] : src.shape[0]],
            dst_ref=dst,
            send_sem=halo_send.at[which],
            recv_sem=halo_recv.at[which],
            device_id={"ctx": lax.rem(me + 1, n_ctx)},
            device_id_type=MESH,
        )

    def state_copy():
        return pltpu.make_async_remote_copy(
            src_ref=state_out,
            dst_ref=state_in,
            send_sem=st_send,
            recv_sem=st_recv,
            device_id={"ctx": lax.rem(me + 1, n_ctx)},
            device_id_type=MESH,
        )

    def attn_copy(r, j):
        part = pl.ds(r * ROWS, ROWS)
        columns = pl.ds(pl.multiple_of(j * PAIR, PAIR), PAIR)
        return pltpu.make_async_remote_copy(
            src_ref=attn_scr.at[part, columns],
            dst_ref=received.at[part, pl.ds(pl.multiple_of(width + j * PAIR, PAIR), PAIR)],
            send_sem=at_send,
            recv_sem=at_recv,
            device_id={"pipe": following},
            device_id_type=MESH,
        )

    def first_copy(i):
        if i < pairs:
            src, dst = tri_out.at[i], tri_in.at[i]
        elif i == pairs:
            src, dst = diag_out, diag_in
        else:
            src, dst = v_hbm.at[pl.ds(0, ROWS)], first_values
        return pltpu.make_async_remote_copy(
            src_ref=src,
            dst_ref=dst,
            send_sem=tri_send.at[max(i - pairs + 1, 0)],
            recv_sem=tri_recv.at[max(i - pairs + 1, 0)],
            device_id={"pipe": following},
            device_id_type=MESH,
        )

    def whole(src, dst, send_sem, recv_sem):
        return pltpu.make_async_remote_copy(
            src_ref=src,
            dst_ref=dst,
            send_sem=send_sem,
            recv_sem=recv_sem,
            device_id={"pipe": following},
            device_id_type=MESH,
        )

    def attn_whole(begin):
        part = pl.ds(begin, rows - begin)
        columns = pl.ds(width, attn_scr.shape[1])
        return whole(attn_scr.at[part], received.at[part, columns], at_send, at_recv)

    def tri_whole():
        return whole(tri_out, tri_in, tri_send.at[0], tri_recv.at[0])

    def mix_whole():
        return whole(mix_scr, received.at[:, pl.ds(0, width)], mx_send, mx_recv)

    def mix_copy(r):
        part = pl.ds(r * ROWS, ROWS)
        return pltpu.make_async_remote_copy(
            src_ref=mix_scr.at[part],
            dst_ref=received.at[part, pl.ds(0, width)],
            send_sem=mx_send,
            recv_sem=mx_recv,
            device_id={"pipe": following},
            device_id_type=MESH,
        )

    row = lax.broadcasted_iota(jnp.int32, (rows, rows), 0)
    col = lax.broadcasted_iota(jnp.int32, (rows, rows), 1)

    pl.semaphore_wait(barrier, n_ctx + 1)

    for d in range(1, n_ctx):

        @pl.when(me + d < n_ctx)
        def _():
            kv_copy(d, 0).start()
            kv_copy(d, 1).start()

    @pl.when(me == 0)
    def _():
        first_copy(pairs + 1).start()

    for which in range(2):
        halo_copy(which).start()

    scale = 1.0 / math.sqrt(ADIM)
    tile_row = lax.broadcasted_iota(jnp.int32, (ROWS, ROWS), 0)
    tile_col = lax.broadcasted_iota(jnp.int32, (ROWS, ROWS), 1)

    def doc_tile(position):
        columns = pl.ds(pl.multiple_of(position, ROWS), ROWS)
        return jnp.broadcast_to(doc_ref[:, columns].astype(jnp.float32), (ROWS, ROWS))

    def make_mask(r, low):
        query_docs = doc_tile(me * rows + r * ROWS).T
        for c in range(low // ROWS, window // ROWS + 1):
            behind = window - c * ROWS
            position = me * rows + r * ROWS - behind
            allowed = doc_tile(jnp.maximum(position, 0)) == query_docs
            if behind == 0:
                allowed = allowed & (tile_row >= tile_col)
            elif behind == window:
                allowed = allowed & (tile_row < tile_col)
            if behind > r * ROWS:
                allowed = allowed & (tile_row * 0 + position >= 0)
            mask_scr[pl.ds(r * ROWS, ROWS), pl.ds(c * ROWS, ROWS)] = jnp.where(allowed, 0.0, -1e30)

    def attend(r, low, begin=False):
        part = pl.ds(r * ROWS, ROWS)
        keys = pl.ds(own + r * ROWS - window + low, window + ROWS - low)

        def pair(j, carry):
            columns = pl.ds(pl.multiple_of(j * PAIR, PAIR), PAIR)
            query = q_ref[part, columns]
            query = jnp.concatenate([query[:, :ADIM], query[:, ADIM:]], axis=0)
            mask = mask_scr[part, low:]
            logits = nt(query, kv_scr[0, keys]) * scale + jnp.concatenate([mask, mask], axis=0)
            probs = jnp.exp(logits - jnp.max(logits, axis=1, keepdims=True))
            total = jnp.sum(probs, axis=1, keepdims=True)
            out = (mm(probs.astype(jnp.bfloat16), kv_scr[1, keys]) / total).astype(jnp.bfloat16)
            attn_scr[part, columns] = jnp.concatenate([out[:ROWS], out[ROWS:]], axis=1)
            attn_copy(r, j).start()
            return carry

        if not begin:
            lax.fori_loop(0, pairs, pair, 0, unroll=True)
            return

        @pl.when(stage >= 0)
        def _():
            pair(0, 0)

        start_rest()
        lax.fori_loop(1, pairs, pair, 0, unroll=True)

    def start_rest():
        for i in late:
            loads[i].start()

    def send_first():
        part = pl.ds(0, ROWS)
        keys = pl.ds(own, ROWS)
        diagonals = []
        for j in range(pairs):
            query = q_ref[part, j * PAIR : (j + 1) * PAIR]
            query = jnp.concatenate([query[:, :ADIM], query[:, ADIM:]], axis=0)
            mask = mask_scr[part, pl.ds(window, ROWS)]
            logits = nt(query, kv_scr[0, keys]) * scale + jnp.concatenate([mask, mask], axis=0)
            probs = jnp.exp(logits - jnp.max(logits, axis=1, keepdims=True))
            probs = probs / jnp.sum(probs, axis=1, keepdims=True)
            second = probs[ROWS:]
            square = jnp.where(tile_row >= tile_col, probs[:ROWS], second.T)
            tri_out[j] = square.astype(jnp.bfloat16)
            first_copy(j).start()
            diagonals.append(
                jnp.sum(jnp.where(tile_row == tile_col, second, 0.0), axis=0, keepdims=True)
            )
        spare = diag_out.shape[0] - pairs
        if spare:
            diagonals.append(jnp.zeros((spare, ROWS), jnp.float32))
        diag_out[...] = jnp.concatenate(diagonals, axis=0)
        first_copy(pairs).start()

    def receive_first():
        tri_whole().wait_recv()
        first_copy(pairs).wait_recv()
        first_copy(pairs + 1).wait_recv()
        values = first_values[...]
        for j in range(pairs):
            square = tri_in[j].astype(jnp.float32)
            diagonal = jnp.where(tile_row == tile_col, diag_in[j : j + 1], 0.0)
            one = jnp.where(tile_row >= tile_col, square, 0.0).astype(jnp.bfloat16)
            two = jnp.where(tile_row < tile_col, square, diagonal).T.astype(jnp.bfloat16)
            both = jnp.concatenate([mm(one, values), mm(two, values)], axis=1)
            received[0:ROWS, width + j * PAIR : width + (j + 1) * PAIR] = both.astype(jnp.bfloat16)

    count = step_ref.shape[0]
    e_row = lax.rem(lax.broadcasted_iota(jnp.int32, (3 * count, width), 0), count)
    e_col = lax.broadcasted_iota(jnp.int32, (3 * count, width), 1) // HDIM
    expand[...] = jnp.where(e_row == e_col, 1.0, 0.0).astype(jnp.bfloat16)

    loads[12].wait()

    @pl.when(me == 0)
    def _():
        loads[10].wait()
        loads[11].wait()
        for r in order:
            make_mask(r, window - r * ROWS)
            loads[queries_at + r].wait()
            if r > 0:
                attend(r, window - r * ROWS, r == order[0])
            else:
                send_first()

    @pl.when(me > 0)
    def _():
        for r in range(blocks):
            make_mask(r, 0)
        loads[10].wait()
        loads[11].wait()
        for d in range(1, n_ctx):

            @pl.when(me - d >= 0)
            def _():
                kv_copy(d, 0).wait_recv()
                kv_copy(d, 1).wait_recv()

            if n_ctx > 2:

                @pl.when(me - d < 0)
                def _():
                    absent = pl.ds(own - d * rows, rows)
                    kv_scr[0, absent] = jnp.zeros((rows, ADIM), jnp.bfloat16)
                    kv_scr[1, absent] = jnp.zeros((rows, ADIM), jnp.bfloat16)

        for r in order:
            loads[queries_at + r].wait()
            attend(r, 0, r == order[0])

    for i in (0, 1, 3, 4, 5, 6, 7, 8):
        loads[i].wait()
    for which in range(2):
        halo_copy(which).wait_recv()
    keep = jnp.where(me > 0, 1.0, 0.0)
    x_ext[0:8] = halo_x[...].astype(jnp.float32)[HALO - 8 :] * keep
    x_ext[8 : 8 + rows] = x_ref[...].astype(jnp.float32)
    bc_ext[0:16] = halo_bc[...].astype(jnp.float32)[2 * HALO - 16 :] * keep
    bc_ext[16 : 16 + 2 * rows] = bc_ref[...].astype(jnp.float32)
    first = 8 - (KERNEL - 1)

    def bc_conv(which):
        total = jnp.zeros((rows, STATE), jnp.float32)
        for tap in range(KERNEL):
            tokens = bc_ext[pl.ds(2 * (first + tap) + which, rows, stride=2)]
            total = total + cbw_ref[tap, which : which + 1] * tokens
        return silu(total)

    b_conv = bc_conv(0)
    c_conv = bc_conv(1)
    gram = jnp.where(row >= col, nt(c_conv, b_conv, highest), 0.0)
    high, low = split2(gram)
    g_hi[...] = high
    g_lo[...] = low
    bt_hi, bt_lo = split2(b_conv.T)
    c_hi, c_lo = split2(c_conv)

    raw = step_ref[...].astype(jnp.float32).T + bias_ref[...]
    step = jnp.maximum(raw, 0.0) + jnp.log1p(jnp.exp(-jnp.abs(raw)))
    log_decay = -rate_ref[...] * step
    lower = jnp.where(row >= col, 1.0, 0.0)
    cumulative = jnp.dot(lower, log_decay, precision=highest, preferred_element_type=jnp.float32)
    grow = split3(jnp.exp(-cumulative) * step)
    fall = split3(jnp.exp(cumulative))
    skip = split3(jnp.broadcast_to(skip_ref[...], (8, count)))

    def prepare(j, carry):
        lanes = pl.ds(pl.multiple_of(j * LANES, LANES), LANES)
        total = cw_ref[0:1, lanes] * x_ext[first : first + rows, lanes]
        for tap in range(1, KERNEL):
            total = total + cw_ref[tap : tap + 1, lanes] * x_ext[first + tap : first + tap + rows, lanes]
        conv = silu(total)
        xc_scr[:, lanes] = conv
        high, low = split2(conv * mm(grow, expand[:, lanes]))
        xt_hi[:, lanes] = high
        xt_lo[:, lanes] = low
        state_acc[:, lanes] = mm(bt_hi, high) + mm(bt_hi, low) + mm(bt_lo, high)
        return carry

    lax.fori_loop(0, width // LANES, prepare, 0, unroll=4)

    @pl.when(me == 0)
    def _():
        state_in[...] = jnp.zeros_like(state_in)

    if n_ctx > 1:

        @pl.when(me > 0)
        def _():
            state_copy().wait_recv()

        @pl.when(me < n_ctx - 1)
        def _():
            end = mm(fall[rows - 16 :], expand[...])[15:16]
            state_out[...] = (end * (state_in[...].astype(jnp.float32) + state_acc[...])).astype(
                jnp.bfloat16
            )
            state_copy().start()

    loads[2].wait()
    loads[9].wait()
    for r in range(blocks):
        part = slice(r * ROWS, (r + 1) * ROWS)
        upto = (r + 1) * ROWS

        def mix_lanes(j, square):
            lanes = pl.ds(pl.multiple_of(j * LANES, LANES), LANES)
            inside = mm(g_hi[part, :upto], xt_hi[:upto, lanes])
            inside = inside + mm(g_hi[part, :upto], xt_lo[:upto, lanes])
            inside = inside + mm(g_lo[part, :upto], xt_hi[:upto, lanes])
            carried = state_in[:, lanes]
            inside = inside + mm(c_hi[part], carried) + mm(c_lo[part], carried)
            e_part = expand[:, lanes]
            out = inside * mm(fall[part], e_part) + mm(skip, e_part)[0:1] * xc_scr[part, lanes]
            out = out * silu(z_ref[part, lanes].astype(jnp.float32))
            gated[:, lanes] = out
            return square + jnp.sum(out * out, axis=1, keepdims=True)

        square = lax.fori_loop(
            0, width // LANES, mix_lanes, jnp.zeros((ROWS, 1), jnp.float32), unroll=4
        )
        norm = lax.rsqrt(square * (1.0 / width) + 1e-05)
        mix_scr[part] = (gated[...] * norm * gain_ref[...]).astype(jnp.bfloat16)
        mix_copy(r).start()

    for d in range(1, n_ctx):

        @pl.when(me + d < n_ctx)
        def _():
            kv_copy(d, 0).wait_send()
            kv_copy(d, 1).wait_send()

    for which in range(2):
        halo_copy(which).wait_send()
    if n_ctx > 1:

        @pl.when(me < n_ctx - 1)
        def _():
            state_copy().wait_send()

    @pl.when(me == 0)
    def _():
        receive_first()
        tri_whole().wait_send()
        first_copy(pairs).wait_send()
        first_copy(pairs + 1).wait_send()
        attn_whole(ROWS).wait()

    @pl.when(me > 0)
    def _():
        attn_whole(0).wait()

    mix_whole().wait()


def store(received, mix_out, attn_out, sem):
    width = mix_out.shape[2]
    copies = [
        pltpu.make_async_copy(received.at[:, pl.ds(0, width)], mix_out.at[0], sem.at[0]),
        pltpu.make_async_copy(
            received.at[:, pl.ds(width, attn_out.shape[2])], attn_out.at[0], sem.at[1]
        ),
    ]
    for copy in copies:
        copy.start()
    for copy in copies:
        copy.wait()


def local(
    mamba_input,
    mamba_bc,
    gate_input,
    step_input,
    step_bias,
    decay_rate,
    skip_gain,
    conv_weight,
    conv_bc_weight,
    norm_gain,
    queries,
    attn_keys,
    attn_values,
    documents,
):
    n_ctx = lax.axis_size("ctx")
    n_pipe = lax.axis_size("pipe")
    _, rows, width = mamba_input.shape
    q_width = queries.shape[2]
    pairs = q_width // PAIR
    blocks = rows // ROWS
    count = step_input.shape[2]
    bf16, f32 = jnp.bfloat16, jnp.float32
    others = max(n_ctx - 1, 1)
    dma = pltpu.SemaphoreType.DMA
    operands = (
        mamba_input[0],
        mamba_bc[0].reshape(2 * rows, STATE),
        gate_input[0],
        step_input[0].T,
        step_bias,
        decay_rate,
        skip_gain,
        conv_weight[0],
        conv_bc_weight[0],
        norm_gain,
        queries[0],
        attn_keys[0],
        attn_values[0],
        documents,
    )
    received = pl.pallas_call(
        functools.partial(kernel, n_ctx, n_pipe),
        out_shape=pltpu.VMEM((rows, width + q_width), bf16),
        in_specs=[pl.BlockSpec(memory_space=pltpu.HBM)] * len(operands),
        out_specs=pl.BlockSpec(memory_space=pltpu.VMEM),
        scratch_shapes=[
            pltpu.VMEM(operand.shape, operand.dtype)
            for operand in operands[:11] + operands[13:]
        ]
        + [
            dma((9 + blocks,)),
            pltpu.VMEM((2, n_ctx * rows, ADIM), bf16),
            pltpu.VMEM((HALO, width), bf16),
            pltpu.VMEM((2 * HALO, STATE), bf16),
            pltpu.VMEM((STATE, width), bf16),
            pltpu.VMEM((STATE, width), bf16),
            pltpu.VMEM((rows, q_width), bf16),
            pltpu.VMEM((rows, width), bf16),
            pltpu.VMEM((rows, documents.shape[1] // 2 + ROWS), f32),
            pltpu.VMEM((3 * count, width), bf16),
            pltpu.VMEM((rows + 8, width), f32),
            pltpu.VMEM((2 * rows + 16, STATE), f32),
            pltpu.VMEM((rows, width), f32),
            pltpu.VMEM((rows, width), bf16),
            pltpu.VMEM((rows, width), bf16),
            pltpu.VMEM((rows, rows), bf16),
            pltpu.VMEM((rows, rows), bf16),
            pltpu.VMEM((STATE, width), f32),
            pltpu.VMEM((ROWS, width), f32),
            dma((2, others)),
            dma((2, others)),
            dma((2,)),
            dma((2,)),
            dma,
            dma,
            pltpu.VMEM((pairs, ROWS, ROWS), bf16),
            pltpu.VMEM((pairs, ROWS, ROWS), bf16),
            pltpu.VMEM((-(-pairs // 8) * 8, ROWS), f32),
            pltpu.VMEM((-(-pairs // 8) * 8, ROWS), f32),
            pltpu.VMEM((ROWS, ADIM), bf16),
            dma,
            dma,
            dma((3,)),
            dma((3,)),
            dma,
            dma,
        ],
        compiler_params=pltpu.CompilerParams(
            collective_id=0, has_side_effects=True, vmem_limit_bytes=50_000_000
        ),
    )(*[pltpu.with_memory_space_constraint(operand, pltpu.HBM) for operand in operands])
    return pl.pallas_call(
        store,
        out_shape=(
            jax.ShapeDtypeStruct(mamba_input.shape, bf16),
            jax.ShapeDtypeStruct(queries.shape, bf16),
        ),
        in_specs=[pl.BlockSpec(memory_space=pltpu.VMEM)],
        out_specs=[pl.BlockSpec(memory_space=pltpu.HBM)] * 2,
        scratch_shapes=[dma((2,))],
        compiler_params=pltpu.CompilerParams(vmem_limit_bytes=50_000_000),
    )(received)


def solution(mesh):
    in_specs = (
        P("pipe", "ctx", "tp"),
        P("pipe", "ctx", None, "tp"),
        P("pipe", "ctx", "tp"),
        P("pipe", "ctx", "tp"),
        P("pipe", "tp"),
        P("pipe", "tp"),
        P("pipe", "tp"),
        P("pipe", None, "tp"),
        P("pipe", None, None, "tp"),
        P("pipe", "tp"),
        P("pipe", "ctx", "tp"),
        P("pipe", "ctx", "tp"),
        P("pipe", "ctx", "tp"),
        P("pipe", None),
    )
    out_specs = (P("pipe", "ctx", "tp"), P("pipe", "ctx", "tp"))
    return jax.shard_map(local, mesh=mesh, in_specs=in_specs, out_specs=out_specs, check_vma=False)
```

```python
import functools
import math

import jax
import jax.numpy as jnp
from jax import lax
from jax.experimental import pallas as pl
from jax.experimental.pallas import tpu as pltpu
from jax.sharding import PartitionSpec as P

HDIM = 64
STATE = 128
KERNEL = 4
ADIM = 128
HALO = 16
LANES = 256
ROWS = 128
PAIR = 2 * ADIM
RELAY = 48
MESH = pl.DeviceIdType.MESH
highest = lax.Precision.HIGHEST


def silu(v):
    half = 0.5 * v
    return half + half * jnp.tanh(half)


def split2(v):
    high = v.astype(jnp.bfloat16)
    return high, (v - high.astype(jnp.float32)).astype(jnp.bfloat16)


def split3(v):
    high = v.astype(jnp.bfloat16)
    rest = v - high.astype(jnp.float32)
    mid = rest.astype(jnp.bfloat16)
    low = (rest - mid.astype(jnp.float32)).astype(jnp.bfloat16)
    return jnp.concatenate([high, mid, low], axis=1)


def mm(a, b):
    return jnp.dot(a, b, preferred_element_type=jnp.float32)


def nt(a, b, precision=None):
    return lax.dot_general(
        a, b, (((1,), (1,)), ((), ())), precision=precision, preferred_element_type=jnp.float32
    )


def kernel(
    n_ctx,
    n_pipe,
    x_hbm,
    bc_hbm,
    z_hbm,
    step_hbm,
    bias_hbm,
    rate_hbm,
    skip_hbm,
    cw_hbm,
    cbw_hbm,
    gain_hbm,
    q_hbm,
    k_hbm,
    v_hbm,
    doc_hbm,
    received,
    x_ref,
    bc_ref,
    z_ref,
    step_ref,
    bias_ref,
    rate_ref,
    skip_ref,
    cw_ref,
    cbw_ref,
    gain_ref,
    q_ref,
    doc_ref,
    load_sem,
    kv_scr,
    halo_x,
    halo_bc,
    state_in,
    state_out,
    attn_scr,
    mix_scr,
    mask_scr,
    expand,
    x_ext,
    bc_ext,
    xc_scr,
    xt_hi,
    xt_lo,
    g_hi,
    g_lo,
    state_acc,
    gated,
    kv_send,
    kv_recv,
    halo_send,
    halo_recv,
    st_send,
    st_recv,
    tri_out,
    tri_in,
    diag_out,
    diag_in,
    first_values,
    at_send,
    at_recv,
    tri_send,
    tri_recv,
    relay_in,
    relay_sem,
    mx_send,
    mx_recv,
):
    me = lax.axis_index("ctx")
    stage = lax.axis_index("pipe")
    following = lax.rem(stage + 1, n_pipe)
    previous = lax.rem(stage + n_pipe - 1, n_pipe)
    rows, width = x_ref.shape
    pairs = q_ref.shape[1] // PAIR
    blocks = rows // ROWS
    window = doc_ref.shape[1] // 2
    own = (n_ctx - 1) * rows
    relayed = n_pipe == 4 and n_ctx == 2 and blocks > 2
    last = n_pipe - 1

    local_keys = pl.ds(own, rows)
    sources = (x_hbm, bc_hbm, z_hbm, step_hbm, bias_hbm, rate_hbm, skip_hbm)
    sources += (cw_hbm, cbw_hbm, gain_hbm, k_hbm, v_hbm, doc_hbm)
    targets = (x_ref, bc_ref, z_ref, step_ref, bias_ref, rate_ref, skip_ref, cw_ref, cbw_ref, gain_ref)
    targets += (kv_scr.at[0, local_keys], kv_scr.at[1, local_keys], doc_ref)
    for r in range(blocks):
        part = pl.ds(r * ROWS, ROWS)
        sources += (q_hbm.at[part],)
        targets += (q_ref.at[part],)
    queries_at = 13
    order = (*range(1, blocks), 0)
    early = (12, 10, queries_at + order[0], 11)
    late = (*(queries_at + r for r in order[1:]), 0, 1, 3, 4, 5, 6, 7, 8, 9, 2)
    slot = {i: k for k, i in enumerate(early)} | {i: k for k, i in enumerate(late)}
    loads = [
        pltpu.make_async_copy(source, target, load_sem.at[slot[i]])
        for i, (source, target) in enumerate(zip(sources, targets))
    ]
    for i in early:
        loads[i].start()

    barrier = pltpu.get_barrier_semaphore()
    pl.semaphore_signal(barrier, inc=1, device_id={"pipe": following}, device_id_type=MESH)
    pl.semaphore_signal(barrier, inc=1, device_id={"pipe": previous}, device_id_type=MESH)
    if relayed:
        opposite = lax.rem(stage + 2, n_pipe)
        pl.semaphore_signal(barrier, inc=1, device_id={"pipe": opposite}, device_id_type=MESH)
    for d in range(1, n_ctx):
        pl.semaphore_signal(
            barrier, inc=1, device_id={"ctx": lax.rem(me + d, n_ctx)}, device_id_type=MESH
        )
    def kv_copy(d, which):
        return pltpu.make_async_remote_copy(
            src_ref=(k_hbm, v_hbm)[which],
            dst_ref=kv_scr.at[which, pl.ds(own - d * rows, rows)],
            send_sem=kv_send.at[which, d - 1],
            recv_sem=kv_recv.at[which, d - 1],
            device_id={"ctx": lax.rem(me + d, n_ctx)},
            device_id_type=MESH,
        )

    def halo_copy(which):
        src, dst = ((x_hbm, halo_x), (bc_hbm, halo_bc))[which]
        return pltpu.make_async_remote_copy(
            src_ref=src.at[src.shape[0] - dst.shape[0] : src.shape[0]],
            dst_ref=dst,
            send_sem=halo_send.at[which],
            recv_sem=halo_recv.at[which],
            device_id={"ctx": lax.rem(me + 1, n_ctx)},
            device_id_type=MESH,
        )

    def state_copy():
        return pltpu.make_async_remote_copy(
            src_ref=state_out,
            dst_ref=state_in,
            send_sem=st_send,
            recv_sem=st_recv,
            device_id={"ctx": lax.rem(me + 1, n_ctx)},
            device_id_type=MESH,
        )

    def attn_copy(r, j):
        part = pl.ds(r * ROWS, ROWS)
        columns = pl.ds(pl.multiple_of(j * PAIR, PAIR), PAIR)
        return pltpu.make_async_remote_copy(
            src_ref=attn_scr.at[part, columns],
            dst_ref=received.at[part, pl.ds(pl.multiple_of(width + j * PAIR, PAIR), PAIR)],
            send_sem=at_send,
            recv_sem=at_recv,
            device_id={"pipe": following},
            device_id_type=MESH,
        )

    def first_copy(i):
        if i < pairs:
            src, dst = tri_out.at[i], tri_in.at[i]
        elif i == pairs:
            src, dst = diag_out, diag_in
        else:
            src, dst = v_hbm.at[pl.ds(0, ROWS)], first_values
        return pltpu.make_async_remote_copy(
            src_ref=src,
            dst_ref=dst,
            send_sem=tri_send.at[max(i - pairs + 1, 0)],
            recv_sem=tri_recv.at[max(i - pairs + 1, 0)],
            device_id={"pipe": following},
            device_id_type=MESH,
        )

    def relay_copy(which):
        first = (blocks - 1) * ROWS
        top, rest = pl.ds(first, RELAY), pl.ds(first + RELAY, ROWS - RELAY)
        pair, columns = pl.ds(0, PAIR), pl.ds(width, PAIR)
        src, dst, target, send_sem, recv_sem = {
            "in": (attn_scr.at[top, pair], relay_in, 1, at_send, relay_sem.at[0]),
            "out": (relay_in, received.at[top, columns], 0, relay_sem.at[1], at_recv),
            "top": (attn_scr.at[top, pair], received.at[top, columns], following, at_send, at_recv),
            "rest": (attn_scr.at[rest, pair], received.at[rest, columns], following, at_send, at_recv),
        }[which]
        return pltpu.make_async_remote_copy(
            src_ref=src,
            dst_ref=dst,
            send_sem=send_sem,
            recv_sem=recv_sem,
            device_id={"pipe": target},
            device_id_type=MESH,
        )

    def send_split():
        @pl.when(stage == last)
        def _():
            relay_copy("in").start()

        @pl.when(stage != last)
        def _():
            relay_copy("top").start()

        relay_copy("rest").start()

    def whole(src, dst, send_sem, recv_sem):
        return pltpu.make_async_remote_copy(
            src_ref=src,
            dst_ref=dst,
            send_sem=send_sem,
            recv_sem=recv_sem,
            device_id={"pipe": following},
            device_id_type=MESH,
        )

    def attn_whole(begin):
        part = pl.ds(begin, rows - begin)
        columns = pl.ds(width, attn_scr.shape[1])
        return whole(attn_scr.at[part], received.at[part, columns], at_send, at_recv)

    def tri_whole():
        return whole(tri_out, tri_in, tri_send.at[0], tri_recv.at[0])

    def mix_whole():
        return whole(mix_scr, received.at[:, pl.ds(0, width)], mx_send, mx_recv)

    def mix_copy(r):
        part = pl.ds(r * ROWS, ROWS)
        return pltpu.make_async_remote_copy(
            src_ref=mix_scr.at[part],
            dst_ref=received.at[part, pl.ds(0, width)],
            send_sem=mx_send,
            recv_sem=mx_recv,
            device_id={"pipe": following},
            device_id_type=MESH,
        )

    row = lax.broadcasted_iota(jnp.int32, (rows, rows), 0)
    col = lax.broadcasted_iota(jnp.int32, (rows, rows), 1)

    pl.semaphore_wait(barrier, n_ctx + (2 if relayed else 1))

    for d in range(1, n_ctx):

        @pl.when(me + d < n_ctx)
        def _():
            kv_copy(d, 0).start()
            kv_copy(d, 1).start()

    @pl.when(me == 0)
    def _():
        first_copy(pairs + 1).start()

    for which in range(2):
        halo_copy(which).start()

    scale = 1.0 / math.sqrt(ADIM)
    tile_row = lax.broadcasted_iota(jnp.int32, (ROWS, ROWS), 0)
    tile_col = lax.broadcasted_iota(jnp.int32, (ROWS, ROWS), 1)

    def doc_tile(position):
        columns = pl.ds(pl.multiple_of(position, ROWS), ROWS)
        return jnp.broadcast_to(doc_ref[:, columns].astype(jnp.float32), (ROWS, ROWS))

    def make_mask(r, low):
        query_docs = doc_tile(me * rows + r * ROWS).T
        for c in range(low // ROWS, window // ROWS + 1):
            behind = window - c * ROWS
            position = me * rows + r * ROWS - behind
            allowed = doc_tile(jnp.maximum(position, 0)) == query_docs
            if behind == 0:
                allowed = allowed & (tile_row >= tile_col)
            elif behind == window:
                allowed = allowed & (tile_row < tile_col)
            if behind > r * ROWS:
                allowed = allowed & (tile_row * 0 + position >= 0)
            mask_scr[pl.ds(r * ROWS, ROWS), pl.ds(c * ROWS, ROWS)] = jnp.where(allowed, 0.0, -1e30)

    def attend(r, low, begin=False):
        split = relayed and r == blocks - 1
        part = pl.ds(r * ROWS, ROWS)
        keys = pl.ds(own + r * ROWS - window + low, window + ROWS - low)

        def pair(j, carry):
            columns = pl.ds(pl.multiple_of(j * PAIR, PAIR), PAIR)
            query = q_ref[part, columns]
            query = jnp.concatenate([query[:, :ADIM], query[:, ADIM:]], axis=0)
            mask = mask_scr[part, low:]
            logits = nt(query, kv_scr[0, keys]) * scale + jnp.concatenate([mask, mask], axis=0)
            probs = jnp.exp(logits - jnp.max(logits, axis=1, keepdims=True))
            total = jnp.sum(probs, axis=1, keepdims=True)
            out = (mm(probs.astype(jnp.bfloat16), kv_scr[1, keys]) / total).astype(jnp.bfloat16)
            attn_scr[part, columns] = jnp.concatenate([out[:ROWS], out[ROWS:]], axis=1)
            if split and isinstance(j, int):
                send_split()
            else:
                attn_copy(r, j).start()
            return carry

        if split:
            pair(0, 0)
        if not begin:
            lax.fori_loop(1 if split else 0, pairs, pair, 0, unroll=True)
            return

        @pl.when(stage >= 0)
        def _():
            pair(0, 0)

        start_rest()
        lax.fori_loop(1, pairs, pair, 0, unroll=True)

    def start_rest():
        for i in late:
            loads[i].start()

    def send_first():
        part = pl.ds(0, ROWS)
        keys = pl.ds(own, ROWS)
        diagonals = []
        for j in range(pairs):
            query = q_ref[part, j * PAIR : (j + 1) * PAIR]
            query = jnp.concatenate([query[:, :ADIM], query[:, ADIM:]], axis=0)
            mask = mask_scr[part, pl.ds(window, ROWS)]
            logits = nt(query, kv_scr[0, keys]) * scale + jnp.concatenate([mask, mask], axis=0)
            probs = jnp.exp(logits - jnp.max(logits, axis=1, keepdims=True))
            probs = probs / jnp.sum(probs, axis=1, keepdims=True)
            second = probs[ROWS:]
            square = jnp.where(tile_row >= tile_col, probs[:ROWS], second.T)
            tri_out[j] = square.astype(jnp.bfloat16)
            first_copy(j).start()
            diagonals.append(
                jnp.sum(jnp.where(tile_row == tile_col, second, 0.0), axis=0, keepdims=True)
            )
        spare = diag_out.shape[0] - pairs
        if spare:
            diagonals.append(jnp.zeros((spare, ROWS), jnp.float32))
        diag_out[...] = jnp.concatenate(diagonals, axis=0)
        first_copy(pairs).start()

    def receive_first():
        tri_whole().wait_recv()
        first_copy(pairs).wait_recv()
        first_copy(pairs + 1).wait_recv()
        values = first_values[...]
        for j in range(pairs):
            square = tri_in[j].astype(jnp.float32)
            diagonal = jnp.where(tile_row == tile_col, diag_in[j : j + 1], 0.0)
            one = jnp.where(tile_row >= tile_col, square, 0.0).astype(jnp.bfloat16)
            two = jnp.where(tile_row < tile_col, square, diagonal).T.astype(jnp.bfloat16)
            both = jnp.concatenate([mm(one, values), mm(two, values)], axis=1)
            received[0:ROWS, width + j * PAIR : width + (j + 1) * PAIR] = both.astype(jnp.bfloat16)

    count = step_ref.shape[0]
    e_row = lax.rem(lax.broadcasted_iota(jnp.int32, (3 * count, width), 0), count)
    e_col = lax.broadcasted_iota(jnp.int32, (3 * count, width), 1) // HDIM
    expand[...] = jnp.where(e_row == e_col, 1.0, 0.0).astype(jnp.bfloat16)

    loads[12].wait()

    @pl.when(me == 0)
    def _():
        loads[10].wait()
        loads[11].wait()
        for r in order:
            make_mask(r, window - r * ROWS)
            loads[queries_at + r].wait()
            if r > 0:
                attend(r, window - r * ROWS, r == order[0])
            else:
                send_first()

    @pl.when(me > 0)
    def _():
        for r in range(blocks):
            make_mask(r, 0)
        loads[10].wait()
        loads[11].wait()
        for d in range(1, n_ctx):

            @pl.when(me - d >= 0)
            def _():
                kv_copy(d, 0).wait_recv()
                kv_copy(d, 1).wait_recv()

            if n_ctx > 2:

                @pl.when(me - d < 0)
                def _():
                    absent = pl.ds(own - d * rows, rows)
                    kv_scr[0, absent] = jnp.zeros((rows, ADIM), jnp.bfloat16)
                    kv_scr[1, absent] = jnp.zeros((rows, ADIM), jnp.bfloat16)

        for r in order:
            loads[queries_at + r].wait()
            attend(r, 0, r == order[0])

    for i in (0, 1, 3, 4, 5, 6, 7, 8):
        loads[i].wait()
    for which in range(2):
        halo_copy(which).wait_recv()
    keep = jnp.where(me > 0, 1.0, 0.0)
    x_ext[0:8] = halo_x[...].astype(jnp.float32)[HALO - 8 :] * keep
    x_ext[8 : 8 + rows] = x_ref[...].astype(jnp.float32)
    bc_ext[0:16] = halo_bc[...].astype(jnp.float32)[2 * HALO - 16 :] * keep
    bc_ext[16 : 16 + 2 * rows] = bc_ref[...].astype(jnp.float32)
    first = 8 - (KERNEL - 1)

    def bc_conv(which):
        total = jnp.zeros((rows, STATE), jnp.float32)
        for tap in range(KERNEL):
            tokens = bc_ext[pl.ds(2 * (first + tap) + which, rows, stride=2)]
            total = total + cbw_ref[tap, which : which + 1] * tokens
        return silu(total)

    b_conv = bc_conv(0)
    c_conv = bc_conv(1)
    gram = jnp.where(row >= col, nt(c_conv, b_conv, highest), 0.0)
    high, low = split2(gram)
    g_hi[...] = high
    g_lo[...] = low
    bt_hi, bt_lo = split2(b_conv.T)
    c_hi, c_lo = split2(c_conv)

    raw = step_ref[...].astype(jnp.float32).T + bias_ref[...]
    step = jnp.maximum(raw, 0.0) + jnp.log1p(jnp.exp(-jnp.abs(raw)))
    log_decay = -rate_ref[...] * step
    lower = jnp.where(row >= col, 1.0, 0.0)
    cumulative = jnp.dot(lower, log_decay, precision=highest, preferred_element_type=jnp.float32)
    grow = split3(jnp.exp(-cumulative) * step)
    fall = split3(jnp.exp(cumulative))
    skip = split3(jnp.broadcast_to(skip_ref[...], (8, count)))

    def prepare(j, carry):
        lanes = pl.ds(pl.multiple_of(j * LANES, LANES), LANES)
        total = cw_ref[0:1, lanes] * x_ext[first : first + rows, lanes]
        for tap in range(1, KERNEL):
            total = total + cw_ref[tap : tap + 1, lanes] * x_ext[first + tap : first + tap + rows, lanes]
        conv = silu(total)
        xc_scr[:, lanes] = conv
        high, low = split2(conv * mm(grow, expand[:, lanes]))
        xt_hi[:, lanes] = high
        xt_lo[:, lanes] = low
        state_acc[:, lanes] = mm(bt_hi, high) + mm(bt_hi, low) + mm(bt_lo, high)
        return carry

    lax.fori_loop(0, width // LANES, prepare, 0, unroll=4)

    @pl.when(me == 0)
    def _():
        state_in[...] = jnp.zeros_like(state_in)

    if n_ctx > 1:

        @pl.when(me > 0)
        def _():
            state_copy().wait_recv()

        @pl.when(me < n_ctx - 1)
        def _():
            end = mm(fall[rows - 16 :], expand[...])[15:16]
            state_out[...] = (end * (state_in[...].astype(jnp.float32) + state_acc[...])).astype(
                jnp.bfloat16
            )
            state_copy().start()

    if relayed:

        @pl.when(stage == 1)
        def _():
            relay_copy("in").wait_recv()
            relay_copy("out").start()

    loads[2].wait()
    loads[9].wait()
    for r in range(blocks):
        part = slice(r * ROWS, (r + 1) * ROWS)
        upto = (r + 1) * ROWS

        def mix_lanes(j, square):
            lanes = pl.ds(pl.multiple_of(j * LANES, LANES), LANES)
            inside = mm(g_hi[part, :upto], xt_hi[:upto, lanes])
            inside = inside + mm(g_hi[part, :upto], xt_lo[:upto, lanes])
            inside = inside + mm(g_lo[part, :upto], xt_hi[:upto, lanes])
            carried = state_in[:, lanes]
            inside = inside + mm(c_hi[part], carried) + mm(c_lo[part], carried)
            e_part = expand[:, lanes]
            out = inside * mm(fall[part], e_part) + mm(skip, e_part)[0:1] * xc_scr[part, lanes]
            out = out * silu(z_ref[part, lanes].astype(jnp.float32))
            gated[:, lanes] = out
            return square + jnp.sum(out * out, axis=1, keepdims=True)

        square = lax.fori_loop(
            0, width // LANES, mix_lanes, jnp.zeros((ROWS, 1), jnp.float32), unroll=4
        )
        norm = lax.rsqrt(square * (1.0 / width) + 1e-05)
        mix_scr[part] = (gated[...] * norm * gain_ref[...]).astype(jnp.bfloat16)
        mix_copy(r).start()

    for d in range(1, n_ctx):

        @pl.when(me + d < n_ctx)
        def _():
            kv_copy(d, 0).wait_send()
            kv_copy(d, 1).wait_send()

    for which in range(2):
        halo_copy(which).wait_send()
    if n_ctx > 1:

        @pl.when(me < n_ctx - 1)
        def _():
            state_copy().wait_send()

    @pl.when(me == 0)
    def _():
        receive_first()
        tri_whole().wait_send()
        first_copy(pairs).wait_send()
        first_copy(pairs + 1).wait_send()
        attn_whole(ROWS).wait()

    @pl.when(me > 0)
    def _():
        attn_whole(0).wait()

    mix_whole().wait()
    if relayed:

        @pl.when(stage == 1)
        def _():
            relay_copy("out").wait_send()


def store(received, mix_out, attn_out, sem):
    width = mix_out.shape[2]
    copies = [
        pltpu.make_async_copy(received.at[:, pl.ds(0, width)], mix_out.at[0], sem.at[0]),
        pltpu.make_async_copy(
            received.at[:, pl.ds(width, attn_out.shape[2])], attn_out.at[0], sem.at[1]
        ),
    ]
    for copy in copies:
        copy.start()
    for copy in copies:
        copy.wait()


def local(
    mamba_input,
    mamba_bc,
    gate_input,
    step_input,
    step_bias,
    decay_rate,
    skip_gain,
    conv_weight,
    conv_bc_weight,
    norm_gain,
    queries,
    attn_keys,
    attn_values,
    documents,
):
    n_ctx = lax.axis_size("ctx")
    n_pipe = lax.axis_size("pipe")
    _, rows, width = mamba_input.shape
    q_width = queries.shape[2]
    pairs = q_width // PAIR
    blocks = rows // ROWS
    count = step_input.shape[2]
    bf16, f32 = jnp.bfloat16, jnp.float32
    others = max(n_ctx - 1, 1)
    dma = pltpu.SemaphoreType.DMA
    operands = (
        mamba_input[0],
        mamba_bc[0].reshape(2 * rows, STATE),
        gate_input[0],
        step_input[0].T,
        step_bias,
        decay_rate,
        skip_gain,
        conv_weight[0],
        conv_bc_weight[0],
        norm_gain,
        queries[0],
        attn_keys[0],
        attn_values[0],
        documents,
    )
    received = pl.pallas_call(
        functools.partial(kernel, n_ctx, n_pipe),
        out_shape=pltpu.VMEM((rows, width + q_width), bf16),
        in_specs=[pl.BlockSpec(memory_space=pltpu.HBM)] * len(operands),
        out_specs=pl.BlockSpec(memory_space=pltpu.VMEM),
        scratch_shapes=[
            pltpu.VMEM(operand.shape, operand.dtype)
            for operand in operands[:11] + operands[13:]
        ]
        + [
            dma((9 + blocks,)),
            pltpu.VMEM((2, n_ctx * rows, ADIM), bf16),
            pltpu.VMEM((HALO, width), bf16),
            pltpu.VMEM((2 * HALO, STATE), bf16),
            pltpu.VMEM((STATE, width), bf16),
            pltpu.VMEM((STATE, width), bf16),
            pltpu.VMEM((rows, q_width), bf16),
            pltpu.VMEM((rows, width), bf16),
            pltpu.VMEM((rows, documents.shape[1] // 2 + ROWS), f32),
            pltpu.VMEM((3 * count, width), bf16),
            pltpu.VMEM((rows + 8, width), f32),
            pltpu.VMEM((2 * rows + 16, STATE), f32),
            pltpu.VMEM((rows, width), f32),
            pltpu.VMEM((rows, width), bf16),
            pltpu.VMEM((rows, width), bf16),
            pltpu.VMEM((rows, rows), bf16),
            pltpu.VMEM((rows, rows), bf16),
            pltpu.VMEM((STATE, width), f32),
            pltpu.VMEM((ROWS, width), f32),
            dma((2, others)),
            dma((2, others)),
            dma((2,)),
            dma((2,)),
            dma,
            dma,
            pltpu.VMEM((pairs, ROWS, ROWS), bf16),
            pltpu.VMEM((pairs, ROWS, ROWS), bf16),
            pltpu.VMEM((-(-pairs // 8) * 8, ROWS), f32),
            pltpu.VMEM((-(-pairs // 8) * 8, ROWS), f32),
            pltpu.VMEM((ROWS, ADIM), bf16),
            dma,
            dma,
            dma((3,)),
            dma((3,)),
            pltpu.VMEM((RELAY, PAIR), bf16),
            dma((2,)),
            dma,
            dma,
        ],
        compiler_params=pltpu.CompilerParams(
            collective_id=0, has_side_effects=True, vmem_limit_bytes=50_000_000
        ),
    )(*[pltpu.with_memory_space_constraint(operand, pltpu.HBM) for operand in operands])
    return pl.pallas_call(
        store,
        out_shape=(
            jax.ShapeDtypeStruct(mamba_input.shape, bf16),
            jax.ShapeDtypeStruct(queries.shape, bf16),
        ),
        in_specs=[pl.BlockSpec(memory_space=pltpu.VMEM)],
        out_specs=[pl.BlockSpec(memory_space=pltpu.HBM)] * 2,
        scratch_shapes=[dma((2,))],
        compiler_params=pltpu.CompilerParams(vmem_limit_bytes=50_000_000),
    )(received)


def solution(mesh):
    in_specs = (
        P("pipe", "ctx", "tp"),
        P("pipe", "ctx", None, "tp"),
        P("pipe", "ctx", "tp"),
        P("pipe", "ctx", "tp"),
        P("pipe", "tp"),
        P("pipe", "tp"),
        P("pipe", "tp"),
        P("pipe", None, "tp"),
        P("pipe", None, None, "tp"),
        P("pipe", "tp"),
        P("pipe", "ctx", "tp"),
        P("pipe", "ctx", "tp"),
        P("pipe", "ctx", "tp"),
        P("pipe", None),
    )
    out_specs = (P("pipe", "ctx", "tp"), P("pipe", "ctx", "tp"))
    return jax.shard_map(local, mesh=mesh, in_specs=in_specs, out_specs=out_specs, check_vma=False)
```

```python
import functools
import math

import jax
import jax.numpy as jnp
from jax import lax
from jax.experimental import pallas as pl
from jax.experimental.pallas import tpu as pltpu
from jax.sharding import PartitionSpec as P

HDIM = 64
STATE = 128
KERNEL = 4
ADIM = 128
HALO = 16
LANES = 256
ROWS = 128
PAIR = 2 * ADIM
RELAY = 48
MESH = pl.DeviceIdType.MESH
highest = lax.Precision.HIGHEST


def silu(v):
    half = 0.5 * v
    return half + half * jnp.tanh(half)


def split2(v):
    high = v.astype(jnp.bfloat16)
    return high, (v - high.astype(jnp.float32)).astype(jnp.bfloat16)


def split3(v):
    high = v.astype(jnp.bfloat16)
    rest = v - high.astype(jnp.float32)
    mid = rest.astype(jnp.bfloat16)
    low = (rest - mid.astype(jnp.float32)).astype(jnp.bfloat16)
    return jnp.concatenate([high, mid, low], axis=1)


def mm(a, b):
    return jnp.dot(a, b, preferred_element_type=jnp.float32)


def nt(a, b, precision=None):
    return lax.dot_general(
        a, b, (((1,), (1,)), ((), ())), precision=precision, preferred_element_type=jnp.float32
    )


def kernel(
    n_ctx,
    n_pipe,
    x_hbm,
    bc_hbm,
    z_hbm,
    step_hbm,
    bias_hbm,
    rate_hbm,
    skip_hbm,
    cw_hbm,
    cbw_hbm,
    gain_hbm,
    q_hbm,
    k_hbm,
    v_hbm,
    doc_hbm,
    received,
    x_ref,
    bc_ref,
    z_ref,
    step_ref,
    bias_ref,
    rate_ref,
    skip_ref,
    cw_ref,
    cbw_ref,
    gain_ref,
    q_ref,
    doc_ref,
    load_sem,
    kv_scr,
    halo_x,
    halo_bc,
    state_in,
    state_out,
    attn_scr,
    mix_scr,
    mask_scr,
    expand,
    x_ext,
    bc_ext,
    xc_scr,
    xt_hi,
    xt_lo,
    g_hi,
    g_lo,
    state_acc,
    gated,
    kv_send,
    kv_recv,
    halo_send,
    halo_recv,
    st_recv,
    tri_out,
    tri_in,
    diag_out,
    diag_in,
    at_send,
    at_recv,
    tri_send,
    tri_recv,
    relay_in,
    relay_sem,
    mx_recv,
):
    me = lax.axis_index("ctx")
    stage = lax.axis_index("pipe")
    following = lax.rem(stage + 1, n_pipe)
    previous = lax.rem(stage + n_pipe - 1, n_pipe)
    rows, width = x_ref.shape
    pairs = q_ref.shape[1] // PAIR
    blocks = rows // ROWS
    window = doc_ref.shape[1] // 2
    own = (n_ctx - 1) * rows
    relayed = n_pipe == 4 and n_ctx == 2 and blocks > 2
    last = n_pipe - 1

    local_keys = pl.ds(own, rows)
    sources = (x_hbm, bc_hbm, z_hbm, step_hbm, bias_hbm, rate_hbm, skip_hbm)
    sources += (cw_hbm, cbw_hbm, gain_hbm, k_hbm, v_hbm, doc_hbm)
    targets = (x_ref, bc_ref, z_ref, step_ref, bias_ref, rate_ref, skip_ref, cw_ref, cbw_ref, gain_ref)
    targets += (kv_scr.at[0, local_keys], kv_scr.at[1, local_keys], doc_ref)
    for r in range(blocks):
        part = pl.ds(r * ROWS, ROWS)
        sources += (q_hbm.at[part],)
        targets += (q_ref.at[part],)
    queries_at = 13
    order = (*range(1, blocks), 0)
    early = (12, 10, queries_at + order[0], 11)
    late = (*(queries_at + r for r in order[1:]), 0, 1, 3, 4, 5, 6, 7, 8, 9, 2)
    slot = {i: k for k, i in enumerate(early)} | {i: k for k, i in enumerate(late)}
    loads = [
        pltpu.make_async_copy(source, target, load_sem.at[slot[i]])
        for i, (source, target) in enumerate(zip(sources, targets))
    ]
    for i in early:
        loads[i].start()

    barrier = pltpu.get_barrier_semaphore()
    pl.semaphore_signal(barrier, inc=1, device_id={"pipe": following}, device_id_type=MESH)
    pl.semaphore_signal(barrier, inc=1, device_id={"pipe": previous}, device_id_type=MESH)
    if relayed:
        opposite = lax.rem(stage + 2, n_pipe)
        pl.semaphore_signal(barrier, inc=1, device_id={"pipe": opposite}, device_id_type=MESH)
    for d in range(1, n_ctx):
        pl.semaphore_signal(
            barrier, inc=1, device_id={"ctx": lax.rem(me + d, n_ctx)}, device_id_type=MESH
        )
    def kv_copy(d, which):
        return pltpu.make_async_remote_copy(
            src_ref=(k_hbm, v_hbm)[which],
            dst_ref=kv_scr.at[which, pl.ds(own - d * rows, rows)],
            send_sem=kv_send.at[d - 1],
            recv_sem=kv_recv.at[d - 1],
            device_id={"ctx": lax.rem(me + d, n_ctx)},
            device_id_type=MESH,
        )

    def kv_whole(d):
        return pltpu.make_async_remote_copy(
            src_ref=kv_scr.at[:, pl.ds(own, rows)],
            dst_ref=kv_scr.at[:, pl.ds(own - d * rows, rows)],
            send_sem=kv_send.at[d - 1],
            recv_sem=kv_recv.at[d - 1],
            device_id={"ctx": lax.rem(me + d, n_ctx)},
            device_id_type=MESH,
        )

    def halo_copy(which):
        src, dst = ((x_hbm, halo_x), (bc_hbm, halo_bc))[which]
        return pltpu.make_async_remote_copy(
            src_ref=src.at[src.shape[0] - dst.shape[0] : src.shape[0]],
            dst_ref=dst,
            send_sem=halo_send.at[which],
            recv_sem=halo_recv.at[which],
            device_id={"ctx": lax.rem(me + 1, n_ctx)},
            device_id_type=MESH,
        )

    def state_copy():
        return pltpu.make_async_remote_copy(
            src_ref=state_out,
            dst_ref=state_in,
            send_sem=load_sem.at[slot[0]],
            recv_sem=st_recv,
            device_id={"ctx": lax.rem(me + 1, n_ctx)},
            device_id_type=MESH,
        )

    def attn_copy(r, j):
        part = pl.ds(r * ROWS, ROWS)
        columns = pl.ds(pl.multiple_of(j * PAIR, PAIR), PAIR)
        return pltpu.make_async_remote_copy(
            src_ref=attn_scr.at[part, columns],
            dst_ref=received.at[part, pl.ds(pl.multiple_of(width + j * PAIR, PAIR), PAIR)],
            send_sem=at_send,
            recv_sem=at_recv,
            device_id={"pipe": following},
            device_id_type=MESH,
        )

    def first_copy(i):
        if i < pairs:
            src, dst = tri_out.at[i], tri_in.at[i]
        elif i == pairs:
            src, dst = diag_out, diag_in
        else:
            src, dst = v_hbm.at[pl.ds(0, ROWS)], tri_in.at[pairs]
        return pltpu.make_async_remote_copy(
            src_ref=src,
            dst_ref=dst,
            send_sem=tri_send.at[1 if i == pairs else 0],
            recv_sem=tri_recv.at[1 if i == pairs else 0],
            device_id={"pipe": following},
            device_id_type=MESH,
        )

    def relay_copy(which):
        first = (blocks - 1) * ROWS
        top, rest = pl.ds(first, RELAY), pl.ds(first + RELAY, ROWS - RELAY)
        pair, columns = pl.ds(0, PAIR), pl.ds(width, PAIR)
        src, dst, target, send_sem, recv_sem = {
            "in": (attn_scr.at[top, pair], relay_in, 1, at_send, relay_sem),
            "out": (relay_in, received.at[top, columns], 0, load_sem.at[slot[1]], at_recv),
            "top": (attn_scr.at[top, pair], received.at[top, columns], following, at_send, at_recv),
            "rest": (attn_scr.at[rest, pair], received.at[rest, columns], following, at_send, at_recv),
        }[which]
        return pltpu.make_async_remote_copy(
            src_ref=src,
            dst_ref=dst,
            send_sem=send_sem,
            recv_sem=recv_sem,
            device_id={"pipe": target},
            device_id_type=MESH,
        )

    def send_split():
        @pl.when(stage == last)
        def _():
            relay_copy("in").start()

        @pl.when(stage != last)
        def _():
            relay_copy("top").start()

        relay_copy("rest").start()

    def whole(src, dst, send_sem, recv_sem):
        return pltpu.make_async_remote_copy(
            src_ref=src,
            dst_ref=dst,
            send_sem=send_sem,
            recv_sem=recv_sem,
            device_id={"pipe": following},
            device_id_type=MESH,
        )

    def attn_whole(begin):
        part = pl.ds(begin, rows - begin)
        columns = pl.ds(width, attn_scr.shape[1])
        return whole(attn_scr.at[part], received.at[part, columns], at_send, at_recv)

    def tri_whole():
        return whole(tri_out, tri_in, tri_send.at[0], tri_recv.at[0])

    def mix_whole():
        return whole(mix_scr, received.at[:, pl.ds(0, width)], load_sem.at[slot[9]], mx_recv)

    def mix_copy(r):
        part = pl.ds(r * ROWS, ROWS)
        return pltpu.make_async_remote_copy(
            src_ref=mix_scr.at[part],
            dst_ref=received.at[part, pl.ds(0, width)],
            send_sem=load_sem.at[slot[9]],
            recv_sem=mx_recv,
            device_id={"pipe": following},
            device_id_type=MESH,
        )

    row = lax.broadcasted_iota(jnp.int32, (rows, rows), 0)
    col = lax.broadcasted_iota(jnp.int32, (rows, rows), 1)

    pl.semaphore_wait(barrier, n_ctx + (2 if relayed else 1))

    for d in range(1, n_ctx):

        @pl.when(me + d < n_ctx)
        def _():
            kv_copy(d, 0).start()
            kv_copy(d, 1).start()

    @pl.when(me == 0)
    def _():
        first_copy(pairs + 1).start()

    for which in range(2):
        halo_copy(which).start()

    scale = 1.0 / math.sqrt(ADIM)
    tile_row = lax.broadcasted_iota(jnp.int32, (ROWS, ROWS), 0)
    tile_col = lax.broadcasted_iota(jnp.int32, (ROWS, ROWS), 1)

    def doc_tile(position):
        columns = pl.ds(pl.multiple_of(position, ROWS), ROWS)
        return jnp.broadcast_to(doc_ref[:, columns].astype(jnp.float32), (ROWS, ROWS))

    def make_mask(r, low):
        query_docs = doc_tile(me * rows + r * ROWS).T
        for c in range(low // ROWS, window // ROWS + 1):
            behind = window - c * ROWS
            position = me * rows + r * ROWS - behind
            allowed = doc_tile(jnp.maximum(position, 0)) == query_docs
            if behind == 0:
                allowed = allowed & (tile_row >= tile_col)
            elif behind == window:
                allowed = allowed & (tile_row < tile_col)
            if behind > r * ROWS:
                allowed = allowed & (tile_row * 0 + position >= 0)
            mask_scr[pl.ds(r * ROWS, ROWS), pl.ds(c * ROWS, ROWS)] = jnp.where(allowed, 0.0, -1e30)

    def attend(r, low, begin=False):
        split = relayed and r == blocks - 1
        part = pl.ds(r * ROWS, ROWS)
        keys = pl.ds(own + r * ROWS - window + low, window + ROWS - low)

        def pair(j, carry):
            columns = pl.ds(pl.multiple_of(j * PAIR, PAIR), PAIR)
            query = q_ref[part, columns]
            query = jnp.concatenate([query[:, :ADIM], query[:, ADIM:]], axis=0)
            mask = mask_scr[part, low:]
            logits = nt(query, kv_scr[0, keys]) * scale + jnp.concatenate([mask, mask], axis=0)
            probs = jnp.exp(logits - jnp.max(logits, axis=1, keepdims=True))
            total = jnp.sum(probs, axis=1, keepdims=True)
            out = (mm(probs.astype(jnp.bfloat16), kv_scr[1, keys]) / total).astype(jnp.bfloat16)
            attn_scr[part, columns] = jnp.concatenate([out[:ROWS], out[ROWS:]], axis=1)
            if split and isinstance(j, int):
                send_split()
            else:
                attn_copy(r, j).start()
            return carry

        if split:
            pair(0, 0)
        if not begin:
            lax.fori_loop(1 if split else 0, pairs, pair, 0, unroll=True)
            return

        @pl.when(stage >= 0)
        def _():
            pair(0, 0)

        start_rest()
        lax.fori_loop(1, pairs, pair, 0, unroll=True)

    def start_rest():
        for i in late:
            loads[i].start(priority=1)

    def send_first():
        part = pl.ds(0, ROWS)
        keys = pl.ds(own, ROWS)
        diagonals = []
        for j in range(pairs):
            query = q_ref[part, j * PAIR : (j + 1) * PAIR]
            query = jnp.concatenate([query[:, :ADIM], query[:, ADIM:]], axis=0)
            mask = mask_scr[part, pl.ds(window, ROWS)]
            logits = nt(query, kv_scr[0, keys]) * scale + jnp.concatenate([mask, mask], axis=0)
            probs = jnp.exp(logits - jnp.max(logits, axis=1, keepdims=True))
            probs = probs / jnp.sum(probs, axis=1, keepdims=True)
            second = probs[ROWS:]
            square = jnp.where(tile_row >= tile_col, probs[:ROWS], second.T)
            tri_out[j] = square.astype(jnp.bfloat16)
            first_copy(j).start()
            diagonals.append(
                jnp.sum(jnp.where(tile_row == tile_col, second, 0.0), axis=0, keepdims=True)
            )
        spare = diag_out.shape[0] - pairs
        if spare:
            diagonals.append(jnp.zeros((spare, ROWS), jnp.float32))
        diag_out[...] = jnp.concatenate(diagonals, axis=0)
        first_copy(pairs).start()

    def receive_first():
        tri_whole().wait_recv()
        first_copy(pairs).wait_recv()
        values = tri_in[pairs]
        for j in range(pairs):
            square = tri_in[j].astype(jnp.float32)
            diagonal = jnp.where(tile_row == tile_col, diag_in[j : j + 1], 0.0)
            one = jnp.where(tile_row >= tile_col, square, 0.0).astype(jnp.bfloat16)
            two = jnp.where(tile_row < tile_col, square, diagonal).T.astype(jnp.bfloat16)
            both = jnp.concatenate([mm(one, values), mm(two, values)], axis=1)
            received[0:ROWS, width + j * PAIR : width + (j + 1) * PAIR] = both.astype(jnp.bfloat16)

    count = step_ref.shape[0]
    e_row = lax.rem(lax.broadcasted_iota(jnp.int32, (3 * count, width), 0), count)
    e_col = lax.broadcasted_iota(jnp.int32, (3 * count, width), 1) // HDIM
    expand[...] = jnp.where(e_row == e_col, 1.0, 0.0).astype(jnp.bfloat16)

    loads[12].wait()

    @pl.when(me == 0)
    def _():
        loads[10].wait()
        loads[11].wait()
        for r in order:
            make_mask(r, window - r * ROWS)
            loads[queries_at + r].wait()
            if r > 0:
                attend(r, window - r * ROWS, r == order[0])
            else:
                send_first()

    @pl.when(me > 0)
    def _():
        for r in range(blocks):
            make_mask(r, 0)
        loads[10].wait()
        loads[11].wait()
        for d in range(1, n_ctx):

            @pl.when(me - d >= 0)
            def _():
                kv_whole(d).wait_recv()

            if n_ctx > 2:

                @pl.when(me - d < 0)
                def _():
                    absent = pl.ds(own - d * rows, rows)
                    kv_scr[0, absent] = jnp.zeros((rows, ADIM), jnp.bfloat16)
                    kv_scr[1, absent] = jnp.zeros((rows, ADIM), jnp.bfloat16)

        for r in order:
            loads[queries_at + r].wait()
            attend(r, 0, r == order[0])

    for i in (0, 1, 3, 4, 5, 6, 7, 8):
        loads[i].wait()
    for which in range(2):
        halo_copy(which).wait_recv()
    keep = jnp.where(me > 0, 1.0, 0.0)
    x_ext[0:8] = halo_x[...].astype(jnp.float32)[HALO - 8 :] * keep
    x_ext[8 : 8 + rows] = x_ref[...].astype(jnp.float32)
    bc_ext[0:16] = halo_bc[...].astype(jnp.float32)[2 * HALO - 16 :] * keep
    bc_ext[16 : 16 + 2 * rows] = bc_ref[...].astype(jnp.float32)
    first = 8 - (KERNEL - 1)

    def bc_conv(which):
        total = jnp.zeros((rows, STATE), jnp.float32)
        for tap in range(KERNEL):
            tokens = bc_ext[pl.ds(2 * (first + tap) + which, rows, stride=2)]
            total = total + cbw_ref[tap, which : which + 1] * tokens
        return silu(total)

    b_conv = bc_conv(0)
    c_conv = bc_conv(1)
    gram = jnp.where(row >= col, nt(c_conv, b_conv, highest), 0.0)
    high, low = split2(gram)
    g_hi[...] = high
    g_lo[...] = low
    bt_hi, bt_lo = split2(b_conv.T)
    c_hi, c_lo = split2(c_conv)

    raw = step_ref[...].astype(jnp.float32).T + bias_ref[...]
    step = jnp.maximum(raw, 0.0) + jnp.log1p(jnp.exp(-jnp.abs(raw)))
    log_decay = -rate_ref[...] * step
    lower = jnp.where(row >= col, 1.0, 0.0)
    cumulative = jnp.dot(lower, log_decay, precision=highest, preferred_element_type=jnp.float32)
    grow = split3(jnp.exp(-cumulative) * step)
    fall = split3(jnp.exp(cumulative))
    skip = split3(jnp.broadcast_to(skip_ref[...], (8, count)))

    def prepare(j, carry):
        lanes = pl.ds(pl.multiple_of(j * LANES, LANES), LANES)
        total = cw_ref[0:1, lanes] * x_ext[first : first + rows, lanes]
        for tap in range(1, KERNEL):
            total = total + cw_ref[tap : tap + 1, lanes] * x_ext[first + tap : first + tap + rows, lanes]
        conv = silu(total)
        xc_scr[:, lanes] = conv
        high, low = split2(conv * mm(grow, expand[:, lanes]))
        xt_hi[:, lanes] = high
        xt_lo[:, lanes] = low
        state_acc[:, lanes] = mm(bt_hi, high) + mm(bt_hi, low) + mm(bt_lo, high)
        return carry

    lax.fori_loop(0, width // LANES, prepare, 0, unroll=4)

    @pl.when(me == 0)
    def _():
        state_in[...] = jnp.zeros_like(state_in)

    if n_ctx > 1:

        @pl.when(me > 0)
        def _():
            state_copy().wait_recv()

        @pl.when(me < n_ctx - 1)
        def _():
            end = mm(fall[rows - 16 :], expand[...])[15:16]
            state_out[...] = (end * (state_in[...].astype(jnp.float32) + state_acc[...])).astype(
                jnp.bfloat16
            )
            state_copy().start()

    if relayed:

        @pl.when(stage == 1)
        def _():
            relay_copy("in").wait_recv()
            relay_copy("out").start()

    loads[2].wait()
    loads[9].wait()
    for r in range(blocks):
        part = slice(r * ROWS, (r + 1) * ROWS)
        upto = (r + 1) * ROWS

        def mix_lanes(j, square):
            lanes = pl.ds(pl.multiple_of(j * LANES, LANES), LANES)
            inside = mm(g_hi[part, :upto], xt_hi[:upto, lanes])
            inside = inside + mm(g_hi[part, :upto], xt_lo[:upto, lanes])
            inside = inside + mm(g_lo[part, :upto], xt_hi[:upto, lanes])
            carried = state_in[:, lanes]
            inside = inside + mm(c_hi[part], carried) + mm(c_lo[part], carried)
            e_part = expand[:, lanes]
            out = inside * mm(fall[part], e_part) + mm(skip, e_part)[0:1] * xc_scr[part, lanes]
            out = out * silu(z_ref[part, lanes].astype(jnp.float32))
            gated[:, lanes] = out
            return square + jnp.sum(out * out, axis=1, keepdims=True)

        square = lax.fori_loop(
            0, width // LANES, mix_lanes, jnp.zeros((ROWS, 1), jnp.float32), unroll=4
        )
        norm = lax.rsqrt(square * (1.0 / width) + 1e-05)
        mix_scr[part] = (gated[...] * norm * gain_ref[...]).astype(jnp.bfloat16)
        mix_copy(r).start()

    for d in range(1, n_ctx):

        @pl.when(me + d < n_ctx)
        def _():
            kv_whole(d).wait_send()

    for which in range(2):
        halo_copy(which).wait_send()
    if n_ctx > 1:

        @pl.when(me < n_ctx - 1)
        def _():
            state_copy().wait_send()

    @pl.when(me == 0)
    def _():
        receive_first()
        tri_whole().wait_send()
        first_copy(pairs).wait_send()
        attn_whole(ROWS).wait()

    @pl.when(me > 0)
    def _():
        attn_whole(0).wait()

    mix_whole().wait()
    if relayed:

        @pl.when(stage == 1)
        def _():
            relay_copy("out").wait_send()


def store(received, mix_out, attn_out, sem):
    width = mix_out.shape[2]
    copies = [
        pltpu.make_async_copy(received.at[:, pl.ds(0, width)], mix_out.at[0], sem.at[0]),
        pltpu.make_async_copy(
            received.at[:, pl.ds(width, attn_out.shape[2])], attn_out.at[0], sem.at[1]
        ),
    ]
    for copy in copies:
        copy.start()
    for copy in copies:
        copy.wait()


def local(
    mamba_input,
    mamba_bc,
    gate_input,
    step_input,
    step_bias,
    decay_rate,
    skip_gain,
    conv_weight,
    conv_bc_weight,
    norm_gain,
    queries,
    attn_keys,
    attn_values,
    documents,
):
    n_ctx = lax.axis_size("ctx")
    n_pipe = lax.axis_size("pipe")
    _, rows, width = mamba_input.shape
    q_width = queries.shape[2]
    pairs = q_width // PAIR
    blocks = rows // ROWS
    count = step_input.shape[2]
    bf16, f32 = jnp.bfloat16, jnp.float32
    others = max(n_ctx - 1, 1)
    dma = pltpu.SemaphoreType.DMA
    operands = (
        mamba_input[0],
        mamba_bc[0].reshape(2 * rows, STATE),
        gate_input[0],
        step_input[0].T,
        step_bias,
        decay_rate,
        skip_gain,
        conv_weight[0],
        conv_bc_weight[0],
        norm_gain,
        queries[0],
        attn_keys[0],
        attn_values[0],
        documents,
    )
    received = pl.pallas_call(
        functools.partial(kernel, n_ctx, n_pipe),
        out_shape=pltpu.VMEM((rows, width + q_width), bf16),
        in_specs=[pl.BlockSpec(memory_space=pltpu.HBM)] * len(operands),
        out_specs=pl.BlockSpec(memory_space=pltpu.VMEM),
        scratch_shapes=[
            pltpu.VMEM(operand.shape, operand.dtype)
            for operand in operands[:11] + operands[13:]
        ]
        + [
            dma((9 + blocks,)),
            pltpu.VMEM((2, n_ctx * rows, ADIM), bf16),
            pltpu.VMEM((HALO, width), bf16),
            pltpu.VMEM((2 * HALO, STATE), bf16),
            pltpu.VMEM((STATE, width), bf16),
            pltpu.VMEM((STATE, width), bf16),
            pltpu.VMEM((rows, q_width), bf16),
            pltpu.VMEM((rows, width), bf16),
            pltpu.VMEM((rows, documents.shape[1] // 2 + ROWS), f32),
            pltpu.VMEM((3 * count, width), bf16),
            pltpu.VMEM((rows + 8, width), f32),
            pltpu.VMEM((2 * rows + 16, STATE), f32),
            pltpu.VMEM((rows, width), f32),
            pltpu.VMEM((rows, width), bf16),
            pltpu.VMEM((rows, width), bf16),
            pltpu.VMEM((rows, rows), bf16),
            pltpu.VMEM((rows, rows), bf16),
            pltpu.VMEM((STATE, width), f32),
            pltpu.VMEM((ROWS, width), f32),
            dma((others,)),
            dma((others,)),
            dma((2,)),
            dma((2,)),
            dma,
            pltpu.VMEM((pairs + 1, ROWS, ROWS), bf16),
            pltpu.VMEM((pairs + 1, ROWS, ROWS), bf16),
            pltpu.VMEM((-(-pairs // 8) * 8, ROWS), f32),
            pltpu.VMEM((-(-pairs // 8) * 8, ROWS), f32),
            dma,
            dma,
            dma((2,)),
            dma((2,)),
            pltpu.VMEM((RELAY, PAIR), bf16),
            dma,
            dma,
        ],
        compiler_params=pltpu.CompilerParams(
            collective_id=0, has_side_effects=True, vmem_limit_bytes=50_000_000
        ),
    )(*[pltpu.with_memory_space_constraint(operand, pltpu.HBM) for operand in operands])
    return pl.pallas_call(
        store,
        out_shape=(
            jax.ShapeDtypeStruct(mamba_input.shape, bf16),
            jax.ShapeDtypeStruct(queries.shape, bf16),
        ),
        in_specs=[pl.BlockSpec(memory_space=pltpu.VMEM)],
        out_specs=[pl.BlockSpec(memory_space=pltpu.HBM)] * 2,
        scratch_shapes=[dma((2,))],
        compiler_params=pltpu.CompilerParams(vmem_limit_bytes=50_000_000),
    )(received)


def solution(mesh):
    in_specs = (
        P("pipe", "ctx", "tp"),
        P("pipe", "ctx", None, "tp"),
        P("pipe", "ctx", "tp"),
        P("pipe", "ctx", "tp"),
        P("pipe", "tp"),
        P("pipe", "tp"),
        P("pipe", "tp"),
        P("pipe", None, "tp"),
        P("pipe", None, None, "tp"),
        P("pipe", "tp"),
        P("pipe", "ctx", "tp"),
        P("pipe", "ctx", "tp"),
        P("pipe", "ctx", "tp"),
        P("pipe", None),
    )
    out_specs = (P("pipe", "ctx", "tp"), P("pipe", "ctx", "tp"))
    return jax.shard_map(local, mesh=mesh, in_specs=in_specs, out_specs=out_specs, check_vma=False)
```

```python
import functools
import math

import jax
import jax.numpy as jnp
from jax import lax
from jax.experimental import pallas as pl
from jax.experimental.pallas import tpu as pltpu
from jax.sharding import PartitionSpec as P

HDIM = 64
STATE = 128
KERNEL = 4
ADIM = 128
HALO = 16
LANES = 256
ROWS = 128
PAIR = 2 * ADIM
RELAY = 48
MESH = pl.DeviceIdType.MESH
highest = lax.Precision.HIGHEST


def silu(v):
    half = 0.5 * v
    return half + half * jnp.tanh(half)


def split2(v):
    high = v.astype(jnp.bfloat16)
    return high, (v - high.astype(jnp.float32)).astype(jnp.bfloat16)


def split3(v):
    high = v.astype(jnp.bfloat16)
    rest = v - high.astype(jnp.float32)
    mid = rest.astype(jnp.bfloat16)
    low = (rest - mid.astype(jnp.float32)).astype(jnp.bfloat16)
    return jnp.concatenate([high, mid, low], axis=1)


def mm(a, b):
    return jnp.dot(a, b, preferred_element_type=jnp.float32)


def nt(a, b, precision=None):
    return lax.dot_general(
        a, b, (((1,), (1,)), ((), ())), precision=precision, preferred_element_type=jnp.float32
    )


def kernel(
    n_ctx,
    n_pipe,
    x_hbm,
    bc_hbm,
    z_hbm,
    step_hbm,
    bias_hbm,
    rate_hbm,
    skip_hbm,
    cw_hbm,
    cbw_hbm,
    gain_hbm,
    q_hbm,
    k_hbm,
    v_hbm,
    doc_hbm,
    received,
    x_ref,
    bc_ref,
    z_ref,
    step_ref,
    bias_ref,
    rate_ref,
    skip_ref,
    cw_ref,
    cbw_ref,
    gain_ref,
    q_ref,
    doc_ref,
    load_sem,
    kv_scr,
    halo_x,
    halo_bc,
    state_in,
    state_out,
    attn_scr,
    mix_scr,
    mask_scr,
    expand,
    x_ext,
    bc_ext,
    xc_scr,
    xt_hi,
    xt_lo,
    g_hi,
    g_lo,
    state_acc,
    gated,
    kv_send,
    kv_recv,
    halo_send,
    halo_recv,
    st_recv,
    tri_out,
    tri_in,
    diag_out,
    diag_in,
    at_send,
    at_recv,
    tri_send,
    tri_recv,
    relay_in,
    relay_sem,
    mx_recv,
):
    me = lax.axis_index("ctx")
    stage = lax.axis_index("pipe")
    following = lax.rem(stage + 1, n_pipe)
    previous = lax.rem(stage + n_pipe - 1, n_pipe)
    rows, width = x_ref.shape
    pairs = q_ref.shape[1] // PAIR
    blocks = rows // ROWS
    window = doc_ref.shape[1] // 2
    own = (n_ctx - 1) * rows
    relayed = n_pipe == 4 and n_ctx == 2 and blocks > 2
    last = n_pipe - 1

    local_keys = pl.ds(own, rows)
    sources = (x_hbm, bc_hbm, z_hbm, step_hbm, bias_hbm, rate_hbm, skip_hbm)
    sources += (cw_hbm, cbw_hbm, gain_hbm, k_hbm, v_hbm, doc_hbm)
    targets = (x_ref, bc_ref, z_ref, step_ref, bias_ref, rate_ref, skip_ref, cw_ref, cbw_ref, gain_ref)
    targets += (kv_scr.at[0, local_keys], kv_scr.at[1, local_keys], doc_ref)
    for r in range(blocks):
        part = pl.ds(r * ROWS, ROWS)
        sources += (q_hbm.at[part],)
        targets += (q_ref.at[part],)
    queries_at = 13
    order = (*range(1, blocks), 0)
    early = (12, 10, queries_at + order[0], 11)
    late = (*(queries_at + r for r in order[1:]), 0, 1, 3, 4, 5, 6, 7, 8, 9, 2)
    slot = {i: k for k, i in enumerate(early)} | {i: k for k, i in enumerate(late)}
    loads = [
        pltpu.make_async_copy(source, target, load_sem.at[slot[i]])
        for i, (source, target) in enumerate(zip(sources, targets))
    ]
    for i in early:
        loads[i].start()

    barrier = pltpu.get_barrier_semaphore()
    pl.semaphore_signal(barrier, inc=1, device_id={"pipe": following}, device_id_type=MESH)
    pl.semaphore_signal(barrier, inc=1, device_id={"pipe": previous}, device_id_type=MESH)
    if relayed:
        opposite = lax.rem(stage + 2, n_pipe)
        pl.semaphore_signal(barrier, inc=1, device_id={"pipe": opposite}, device_id_type=MESH)
    for d in range(1, n_ctx):
        pl.semaphore_signal(
            barrier, inc=1, device_id={"ctx": lax.rem(me + d, n_ctx)}, device_id_type=MESH
        )
    def kv_copy(d, which):
        return pltpu.make_async_remote_copy(
            src_ref=(k_hbm, v_hbm)[which],
            dst_ref=kv_scr.at[which, pl.ds(own - d * rows, rows)],
            send_sem=kv_send.at[d - 1],
            recv_sem=kv_recv.at[d - 1],
            device_id={"ctx": lax.rem(me + d, n_ctx)},
            device_id_type=MESH,
        )

    def kv_whole(d):
        return pltpu.make_async_remote_copy(
            src_ref=kv_scr.at[:, pl.ds(own, rows)],
            dst_ref=kv_scr.at[:, pl.ds(own - d * rows, rows)],
            send_sem=kv_send.at[d - 1],
            recv_sem=kv_recv.at[d - 1],
            device_id={"ctx": lax.rem(me + d, n_ctx)},
            device_id_type=MESH,
        )

    def halo_copy(which):
        src, dst = ((x_hbm, halo_x), (bc_hbm, halo_bc))[which]
        return pltpu.make_async_remote_copy(
            src_ref=src.at[src.shape[0] - dst.shape[0] : src.shape[0]],
            dst_ref=dst,
            send_sem=halo_send.at[which],
            recv_sem=halo_recv.at[which],
            device_id={"ctx": lax.rem(me + 1, n_ctx)},
            device_id_type=MESH,
        )

    def state_copy():
        return pltpu.make_async_remote_copy(
            src_ref=state_out,
            dst_ref=state_in,
            send_sem=load_sem.at[slot[0]],
            recv_sem=st_recv,
            device_id={"ctx": lax.rem(me + 1, n_ctx)},
            device_id_type=MESH,
        )

    def attn_copy(r, j):
        part = pl.ds(r * ROWS, ROWS)
        columns = pl.ds(pl.multiple_of(j * PAIR, PAIR), PAIR)
        return pltpu.make_async_remote_copy(
            src_ref=attn_scr.at[part, columns],
            dst_ref=received.at[part, pl.ds(pl.multiple_of(width + j * PAIR, PAIR), PAIR)],
            send_sem=at_send,
            recv_sem=at_recv,
            device_id={"pipe": following},
            device_id_type=MESH,
        )

    def first_copy(i):
        if i < pairs:
            src, dst = tri_out.at[i], tri_in.at[i]
        elif i == pairs:
            src, dst = diag_out, diag_in
        else:
            src, dst = v_hbm.at[pl.ds(0, ROWS)], tri_in.at[pairs]
        return pltpu.make_async_remote_copy(
            src_ref=src,
            dst_ref=dst,
            send_sem=tri_send.at[1 if i == pairs else 0],
            recv_sem=tri_recv.at[1 if i == pairs else 0],
            device_id={"pipe": following},
            device_id_type=MESH,
        )

    def relay_copy(which):
        first = (blocks - 1) * ROWS
        top, rest = pl.ds(first, RELAY), pl.ds(first + RELAY, ROWS - RELAY)
        pair, columns = pl.ds(0, PAIR), pl.ds(width, PAIR)
        src, dst, target, send_sem, recv_sem = {
            "in": (attn_scr.at[top, pair], relay_in, 1, at_send, relay_sem),
            "out": (relay_in, received.at[top, columns], 0, load_sem.at[slot[1]], at_recv),
            "top": (attn_scr.at[top, pair], received.at[top, columns], following, at_send, at_recv),
            "rest": (attn_scr.at[rest, pair], received.at[rest, columns], following, at_send, at_recv),
        }[which]
        return pltpu.make_async_remote_copy(
            src_ref=src,
            dst_ref=dst,
            send_sem=send_sem,
            recv_sem=recv_sem,
            device_id={"pipe": target},
            device_id_type=MESH,
        )

    def send_split():
        @pl.when(stage == last)
        def _():
            relay_copy("in").start()

        @pl.when(stage != last)
        def _():
            relay_copy("top").start()

        relay_copy("rest").start()

    def whole(src, dst, send_sem, recv_sem):
        return pltpu.make_async_remote_copy(
            src_ref=src,
            dst_ref=dst,
            send_sem=send_sem,
            recv_sem=recv_sem,
            device_id={"pipe": following},
            device_id_type=MESH,
        )

    def attn_whole(begin):
        part = pl.ds(begin, rows - begin)
        columns = pl.ds(width, attn_scr.shape[1])
        return whole(attn_scr.at[part], received.at[part, columns], at_send, at_recv)

    def tri_whole():
        return whole(tri_out, tri_in, tri_send.at[0], tri_recv.at[0])

    def mix_whole():
        return whole(mix_scr, received.at[:, pl.ds(0, width)], load_sem.at[slot[9]], mx_recv)

    def mix_copy(r):
        part = pl.ds(r * ROWS, ROWS)
        return pltpu.make_async_remote_copy(
            src_ref=mix_scr.at[part],
            dst_ref=received.at[part, pl.ds(0, width)],
            send_sem=load_sem.at[slot[9]],
            recv_sem=mx_recv,
            device_id={"pipe": following},
            device_id_type=MESH,
        )

    row = lax.broadcasted_iota(jnp.int32, (rows, rows), 0)
    col = lax.broadcasted_iota(jnp.int32, (rows, rows), 1)

    pl.semaphore_wait(barrier, n_ctx + (2 if relayed else 1))

    for d in range(1, n_ctx):

        @pl.when(me + d < n_ctx)
        def _():
            kv_copy(d, 0).start()
            kv_copy(d, 1).start()

    @pl.when(me == 0)
    def _():
        first_copy(pairs + 1).start()

    @pl.when(me < n_ctx - 1)
    def _():
        for which in range(2):
            halo_copy(which).start()

    scale = 1.0 / math.sqrt(ADIM)
    tile_row = lax.broadcasted_iota(jnp.int32, (ROWS, ROWS), 0)
    tile_col = lax.broadcasted_iota(jnp.int32, (ROWS, ROWS), 1)

    def doc_tile(position):
        columns = pl.ds(pl.multiple_of(position, ROWS), ROWS)
        return jnp.broadcast_to(doc_ref[:, columns].astype(jnp.float32), (ROWS, ROWS))

    def make_mask(r, low):
        query_docs = doc_tile(me * rows + r * ROWS).T
        for c in range(low // ROWS, window // ROWS + 1):
            behind = window - c * ROWS
            position = me * rows + r * ROWS - behind
            allowed = doc_tile(jnp.maximum(position, 0)) == query_docs
            if behind == 0:
                allowed = allowed & (tile_row >= tile_col)
            elif behind == window:
                allowed = allowed & (tile_row < tile_col)
            if behind > r * ROWS:
                allowed = allowed & (tile_row * 0 + position >= 0)
            mask_scr[pl.ds(r * ROWS, ROWS), pl.ds(c * ROWS, ROWS)] = jnp.where(allowed, 0.0, -1e30)

    def attend(r, low, begin=False):
        split = relayed and r == blocks - 1
        part = pl.ds(r * ROWS, ROWS)
        keys = pl.ds(own + r * ROWS - window + low, window + ROWS - low)

        def pair(j, carry):
            columns = pl.ds(pl.multiple_of(j * PAIR, PAIR), PAIR)
            query = q_ref[part, columns]
            query = jnp.concatenate([query[:, :ADIM], query[:, ADIM:]], axis=0)
            mask = mask_scr[part, low:]
            logits = nt(query, kv_scr[0, keys]) * scale + jnp.concatenate([mask, mask], axis=0)
            probs = jnp.exp(logits - jnp.max(logits, axis=1, keepdims=True))
            total = jnp.sum(probs, axis=1, keepdims=True)
            out = (mm(probs.astype(jnp.bfloat16), kv_scr[1, keys]) / total).astype(jnp.bfloat16)
            attn_scr[part, columns] = jnp.concatenate([out[:ROWS], out[ROWS:]], axis=1)
            if split and isinstance(j, int):
                send_split()
            else:
                attn_copy(r, j).start()
            return carry

        if split:
            pair(0, 0)
        if not begin:
            lax.fori_loop(1 if split else 0, pairs, pair, 0, unroll=True)
            return

        @pl.when(stage >= 0)
        def _():
            pair(0, 0)

        start_rest()
        lax.fori_loop(1, pairs, pair, 0, unroll=True)

    def start_rest():
        for i in late:
            loads[i].start(priority=1)

    def send_first():
        part = pl.ds(0, ROWS)
        keys = pl.ds(own, ROWS)
        diagonals = []
        for j in range(pairs):
            query = q_ref[part, j * PAIR : (j + 1) * PAIR]
            query = jnp.concatenate([query[:, :ADIM], query[:, ADIM:]], axis=0)
            mask = mask_scr[part, pl.ds(window, ROWS)]
            logits = nt(query, kv_scr[0, keys]) * scale + jnp.concatenate([mask, mask], axis=0)
            probs = jnp.exp(logits - jnp.max(logits, axis=1, keepdims=True))
            probs = probs / jnp.sum(probs, axis=1, keepdims=True)
            second = probs[ROWS:]
            square = jnp.where(tile_row >= tile_col, probs[:ROWS], second.T)
            tri_out[j] = square.astype(jnp.bfloat16)
            first_copy(j).start()
            diagonals.append(
                jnp.sum(jnp.where(tile_row == tile_col, second, 0.0), axis=0, keepdims=True)
            )
        spare = diag_out.shape[0] - pairs
        if spare:
            diagonals.append(jnp.zeros((spare, ROWS), jnp.float32))
        diag_out[...] = jnp.concatenate(diagonals, axis=0)
        first_copy(pairs).start()

    def receive_first():
        tri_whole().wait_recv()
        first_copy(pairs).wait_recv()
        values = tri_in[pairs]
        for j in range(pairs):
            square = tri_in[j].astype(jnp.float32)
            diagonal = jnp.where(tile_row == tile_col, diag_in[j : j + 1], 0.0)
            one = jnp.where(tile_row >= tile_col, square, 0.0).astype(jnp.bfloat16)
            two = jnp.where(tile_row < tile_col, square, diagonal).T.astype(jnp.bfloat16)
            both = jnp.concatenate([mm(one, values), mm(two, values)], axis=1)
            received[0:ROWS, width + j * PAIR : width + (j + 1) * PAIR] = both.astype(jnp.bfloat16)

    count = step_ref.shape[0]
    e_row = lax.rem(lax.broadcasted_iota(jnp.int32, (3 * count, width), 0), count)
    e_col = lax.broadcasted_iota(jnp.int32, (3 * count, width), 1) // HDIM
    expand[...] = jnp.where(e_row == e_col, 1.0, 0.0).astype(jnp.bfloat16)

    loads[12].wait()

    @pl.when(me == 0)
    def _():
        loads[10].wait()
        loads[11].wait()
        for r in order:
            make_mask(r, window - r * ROWS)
            loads[queries_at + r].wait()
            if r > 0:
                attend(r, window - r * ROWS, r == order[0])
            else:
                send_first()

    @pl.when(me > 0)
    def _():
        for r in range(blocks):
            make_mask(r, 0)
        loads[10].wait()
        loads[11].wait()
        for d in range(1, n_ctx):

            @pl.when(me - d >= 0)
            def _():
                kv_whole(d).wait_recv()

            if n_ctx > 2:

                @pl.when(me - d < 0)
                def _():
                    absent = pl.ds(own - d * rows, rows)
                    kv_scr[0, absent] = jnp.zeros((rows, ADIM), jnp.bfloat16)
                    kv_scr[1, absent] = jnp.zeros((rows, ADIM), jnp.bfloat16)

        for r in order:
            loads[queries_at + r].wait()
            attend(r, 0, r == order[0])

    for i in (0, 1, 3, 4, 5, 6, 7, 8):
        loads[i].wait()
    @pl.when(me > 0)
    def _():
        for which in range(2):
            halo_copy(which).wait_recv()

    @pl.when(me == 0)
    def _():
        halo_x[...] = jnp.zeros_like(halo_x)
        halo_bc[...] = jnp.zeros_like(halo_bc)

    x_ext[0:8] = halo_x[...].astype(jnp.float32)[HALO - 8 :]
    x_ext[8 : 8 + rows] = x_ref[...].astype(jnp.float32)
    bc_ext[0:16] = halo_bc[...].astype(jnp.float32)[2 * HALO - 16 :]
    bc_ext[16 : 16 + 2 * rows] = bc_ref[...].astype(jnp.float32)
    first = 8 - (KERNEL - 1)

    def bc_conv(which):
        total = jnp.zeros((rows, STATE), jnp.float32)
        for tap in range(KERNEL):
            tokens = bc_ext[pl.ds(2 * (first + tap) + which, rows, stride=2)]
            total = total + cbw_ref[tap, which : which + 1] * tokens
        return silu(total)

    b_conv = bc_conv(0)
    c_conv = bc_conv(1)
    gram = jnp.where(row >= col, nt(c_conv, b_conv, highest), 0.0)
    high, low = split2(gram)
    g_hi[...] = high
    g_lo[...] = low
    bt_hi, bt_lo = split2(b_conv.T)
    c_hi, c_lo = split2(c_conv)

    raw = step_ref[...].astype(jnp.float32).T + bias_ref[...]
    step = jnp.maximum(raw, 0.0) + jnp.log1p(jnp.exp(-jnp.abs(raw)))
    log_decay = -rate_ref[...] * step
    lower = jnp.where(row >= col, 1.0, 0.0)
    cumulative = jnp.dot(lower, log_decay, precision=highest, preferred_element_type=jnp.float32)
    grow = split3(jnp.exp(-cumulative) * step)
    fall = split3(jnp.exp(cumulative))
    skip = split3(jnp.broadcast_to(skip_ref[...], (8, count)))

    def prepare(j, carry):
        lanes = pl.ds(pl.multiple_of(j * LANES, LANES), LANES)
        total = cw_ref[0:1, lanes] * x_ext[first : first + rows, lanes]
        for tap in range(1, KERNEL):
            total = total + cw_ref[tap : tap + 1, lanes] * x_ext[first + tap : first + tap + rows, lanes]
        conv = silu(total)
        xc_scr[:, lanes] = conv
        high, low = split2(conv * mm(grow, expand[:, lanes]))
        xt_hi[:, lanes] = high
        xt_lo[:, lanes] = low
        state_acc[:, lanes] = mm(bt_hi, high) + mm(bt_hi, low) + mm(bt_lo, high)
        return carry

    lax.fori_loop(0, width // LANES, prepare, 0, unroll=4)

    @pl.when(me == 0)
    def _():
        state_in[...] = jnp.zeros_like(state_in)

    if n_ctx > 1:

        @pl.when(me > 0)
        def _():
            state_copy().wait_recv()

        @pl.when(me < n_ctx - 1)
        def _():
            end = mm(fall[rows - 16 :], expand[...])[15:16]
            state_out[...] = (end * (state_in[...].astype(jnp.float32) + state_acc[...])).astype(
                jnp.bfloat16
            )
            state_copy().start()

    if relayed:

        @pl.when(stage == 1)
        def _():
            relay_copy("in").wait_recv()
            relay_copy("out").start()

    loads[2].wait()
    loads[9].wait()
    for r in range(blocks):
        part = slice(r * ROWS, (r + 1) * ROWS)
        upto = (r + 1) * ROWS

        def mix_lanes(j, square):
            lanes = pl.ds(pl.multiple_of(j * LANES, LANES), LANES)
            inside = mm(g_hi[part, :upto], xt_hi[:upto, lanes])
            inside = inside + mm(g_hi[part, :upto], xt_lo[:upto, lanes])
            inside = inside + mm(g_lo[part, :upto], xt_hi[:upto, lanes])
            carried = state_in[:, lanes]
            inside = inside + mm(c_hi[part], carried) + mm(c_lo[part], carried)
            e_part = expand[:, lanes]
            out = inside * mm(fall[part], e_part) + mm(skip, e_part)[0:1] * xc_scr[part, lanes]
            out = out * silu(z_ref[part, lanes].astype(jnp.float32))
            gated[:, lanes] = out
            return square + jnp.sum(out * out, axis=1, keepdims=True)

        square = lax.fori_loop(
            0, width // LANES, mix_lanes, jnp.zeros((ROWS, 1), jnp.float32), unroll=4
        )
        norm = lax.rsqrt(square * (1.0 / width) + 1e-05)
        mix_scr[part] = (gated[...] * norm * gain_ref[...]).astype(jnp.bfloat16)
        mix_copy(r).start()

    for d in range(1, n_ctx):

        @pl.when(me + d < n_ctx)
        def _():
            kv_whole(d).wait_send()

    @pl.when(me < n_ctx - 1)
    def _():
        for which in range(2):
            halo_copy(which).wait_send()

    if n_ctx > 1:

        @pl.when(me < n_ctx - 1)
        def _():
            state_copy().wait_send()

    @pl.when(me == 0)
    def _():
        receive_first()
        tri_whole().wait_send()
        first_copy(pairs).wait_send()
        attn_whole(ROWS).wait()

    @pl.when(me > 0)
    def _():
        attn_whole(0).wait()

    mix_whole().wait()
    if relayed:

        @pl.when(stage == 1)
        def _():
            relay_copy("out").wait_send()


def store(received, mix_out, attn_out, sem):
    width = mix_out.shape[2]
    copies = [
        pltpu.make_async_copy(received.at[:, pl.ds(0, width)], mix_out.at[0], sem.at[0]),
        pltpu.make_async_copy(
            received.at[:, pl.ds(width, attn_out.shape[2])], attn_out.at[0], sem.at[1]
        ),
    ]
    for copy in copies:
        copy.start()
    for copy in copies:
        copy.wait()


def local(
    mamba_input,
    mamba_bc,
    gate_input,
    step_input,
    step_bias,
    decay_rate,
    skip_gain,
    conv_weight,
    conv_bc_weight,
    norm_gain,
    queries,
    attn_keys,
    attn_values,
    documents,
):
    n_ctx = lax.axis_size("ctx")
    n_pipe = lax.axis_size("pipe")
    _, rows, width = mamba_input.shape
    q_width = queries.shape[2]
    pairs = q_width // PAIR
    blocks = rows // ROWS
    count = step_input.shape[2]
    bf16, f32 = jnp.bfloat16, jnp.float32
    others = max(n_ctx - 1, 1)
    dma = pltpu.SemaphoreType.DMA
    operands = (
        mamba_input[0],
        mamba_bc[0].reshape(2 * rows, STATE),
        gate_input[0],
        step_input[0].T,
        step_bias,
        decay_rate,
        skip_gain,
        conv_weight[0],
        conv_bc_weight[0],
        norm_gain,
        queries[0],
        attn_keys[0],
        attn_values[0],
        documents,
    )
    received = pl.pallas_call(
        functools.partial(kernel, n_ctx, n_pipe),
        out_shape=pltpu.VMEM((rows, width + q_width), bf16),
        in_specs=[pl.BlockSpec(memory_space=pltpu.HBM)] * len(operands),
        out_specs=pl.BlockSpec(memory_space=pltpu.VMEM),
        scratch_shapes=[
            pltpu.VMEM(operand.shape, operand.dtype)
            for operand in operands[:11] + operands[13:]
        ]
        + [
            dma((9 + blocks,)),
            pltpu.VMEM((2, n_ctx * rows, ADIM), bf16),
            pltpu.VMEM((HALO, width), bf16),
            pltpu.VMEM((2 * HALO, STATE), bf16),
            pltpu.VMEM((STATE, width), bf16),
            pltpu.VMEM((STATE, width), bf16),
            pltpu.VMEM((rows, q_width), bf16),
            pltpu.VMEM((rows, width), bf16),
            pltpu.VMEM((rows, documents.shape[1] // 2 + ROWS), f32),
            pltpu.VMEM((3 * count, width), bf16),
            pltpu.VMEM((rows + 8, width), f32),
            pltpu.VMEM((2 * rows + 16, STATE), f32),
            pltpu.VMEM((rows, width), f32),
            pltpu.VMEM((rows, width), bf16),
            pltpu.VMEM((rows, width), bf16),
            pltpu.VMEM((rows, rows), bf16),
            pltpu.VMEM((rows, rows), bf16),
            pltpu.VMEM((STATE, width), f32),
            pltpu.VMEM((ROWS, width), f32),
            dma((others,)),
            dma((others,)),
            dma((2,)),
            dma((2,)),
            dma,
            pltpu.VMEM((pairs + 1, ROWS, ROWS), bf16),
            pltpu.VMEM((pairs + 1, ROWS, ROWS), bf16),
            pltpu.VMEM((-(-pairs // 8) * 8, ROWS), f32),
            pltpu.VMEM((-(-pairs // 8) * 8, ROWS), f32),
            dma,
            dma,
            dma((2,)),
            dma((2,)),
            pltpu.VMEM((RELAY, PAIR), bf16),
            dma,
            dma,
        ],
        compiler_params=pltpu.CompilerParams(
            collective_id=0, has_side_effects=True, vmem_limit_bytes=50_000_000
        ),
    )(*[pltpu.with_memory_space_constraint(operand, pltpu.HBM) for operand in operands])
    return pl.pallas_call(
        store,
        out_shape=(
            jax.ShapeDtypeStruct(mamba_input.shape, bf16),
            jax.ShapeDtypeStruct(queries.shape, bf16),
        ),
        in_specs=[pl.BlockSpec(memory_space=pltpu.VMEM)],
        out_specs=[pl.BlockSpec(memory_space=pltpu.HBM)] * 2,
        scratch_shapes=[dma((2,))],
        compiler_params=pltpu.CompilerParams(vmem_limit_bytes=50_000_000),
    )(received)


def solution(mesh):
    in_specs = (
        P("pipe", "ctx", "tp"),
        P("pipe", "ctx", None, "tp"),
        P("pipe", "ctx", "tp"),
        P("pipe", "ctx", "tp"),
        P("pipe", "tp"),
        P("pipe", "tp"),
        P("pipe", "tp"),
        P("pipe", None, "tp"),
        P("pipe", None, None, "tp"),
        P("pipe", "tp"),
        P("pipe", "ctx", "tp"),
        P("pipe", "ctx", "tp"),
        P("pipe", "ctx", "tp"),
        P("pipe", None),
    )
    out_specs = (P("pipe", "ctx", "tp"), P("pipe", "ctx", "tp"))
    return jax.shard_map(local, mesh=mesh, in_specs=in_specs, out_specs=out_specs, check_vma=False)
```
